32 devices in a mesh: groups: 2 (over x), seq: 16 (over z, y, core).
Axes of the slice: x: 2, y: 2, z: 4, core: 2. Of those that a mesh axis runs over, the one named last changes fastest.
Arguments:
- inputs: bfloat16 [2, 32768, 256], P('groups', 'seq'), parts along dimension 0, may hold values from -6 to 6
- cotangent: bfloat16 [2, 32768, 256], P('groups', 'seq'), parts along dimension 0, may hold values from -6 to 6
- taps_first: bfloat16 [3, 256, 256], replicated, may hold values from -0.21875 to 0.21875
- taps_second: bfloat16 [3, 256, 256], replicated, may hold values from -0.21875 to 0.21875
- bias_first: float32 [256], replicated, may hold values from -3 to 3
- bias_second: float32 [256], replicated, may hold values from -3 to 3
- proj_first: bfloat16 [256, 256], replicated, may hold values from -0.375 to 0.375
- proj_second: bfloat16 [256, 256], replicated, may hold values from -0.375 to 0.375
- gain_first: float32 [256], replicated, may hold values from 0.2 to 1.8
- gain_second: float32 [256], replicated, may hold values from 0.2 to 1.8
Outputs:
- outputs: bfloat16 [2, 32768, 256], P('groups', 'seq'), parts along dimension 0
- input_grad: bfloat16 [2, 32768, 256], P('groups', 'seq'), parts along dimension 0
- taps_grad_first: float32 [6, 256, 256], P('groups'), parts along dimension 0
- taps_grad_second: float32 [6, 256, 256], P('groups'), parts along dimension 0
- proj_grad_first: float32 [512, 256], P('groups'), parts along dimension 0
- proj_grad_second: float32 [512, 256], P('groups'), parts along dimension 0
The draws below stay inside these ranges and needn't reach their ends.
There are 2 independent parts, one for each index of `groups`. The reference program is written for one: setup_inputs(seed, part) draws one part's arguments, and reference() takes and returns one part's arrays. A program takes and returns all parts, laid end to end along the dimension named above; an argument that names none is the same for every part. Nothing has to cross between parts.
All inputs are finite; a program needn't handle non-finite values.
Results may differ from the reference program's by a relative error of at most 0.0068.
Values may be sent and summed in bfloat16 or wider, within the bound.
No kernel may reach another device: no remote copies, remote signals or barrier semaphores. Data moves between devices by JAX's collectives and lax.ppermute only.
A program may use at most 64 MiB of HBM per device.

```python
import jax
import jax.numpy as jnp
from jax import lax

C = 256
POS_DEV = 2048
WINDOWS = 1
HOP1 = 4
HOP2 = 8
LEN = 32768


def level_of(rng, shape, shards, smallest, largest):
    def one(position, shards_of):
        draws = jax.random.uniform(jax.random.fold_in(jax.random.fold_in(rng, 6), position), (shards_of,), jnp.float32, smallest / len(shards), largest / len(shards))
        return jnp.repeat(jnp.exp(draws), shape[position] // shards_of).reshape((-1,) + (1,) * (len(shape) - position - 1))

    factor_of = one(*shards[0])
    for cut in shards[1:]:
        factor_of = factor_of * one(*cut)
    return factor_of


def gaussian(key, shape, spread, limit, split=(), kind=jnp.bfloat16):
    values = jax.random.normal(key, shape, jnp.float32) * spread
    if len(split) > 0:
        values = level_of(key, shape, split, -0.22, 0.18) * values
    return jnp.clip(values, min=-limit, max=limit).astype(kind)


def setup_inputs(seed: int = 0, part: int = 0) -> dict:
    key_list = jax.random.split(jax.random.key(seed), 11)
    own_keys = jax.random.split(jax.random.fold_in(key_list[10], part), 11)
    inputs = gaussian(own_keys[0], (WINDOWS, LEN, C), 1.0, 6.0, ((1, 16),))
    cotangent = gaussian(own_keys[1], (WINDOWS, LEN, C), 1.0, 6.0, ((1, 16),))
    taps_first = gaussian(key_list[2], (3, C, C), (3 * C) ** -0.5, 0.21875)
    taps_second = gaussian(key_list[3], (3, C, C), (3 * C) ** -0.5, 0.21875)
    bias_first = gaussian(key_list[4], (C,), 0.5, 3.0, (), jnp.float32)
    bias_second = gaussian(key_list[5], (C,), 0.5, 3.0, (), jnp.float32)
    proj_first = gaussian(key_list[6], (C, C), C ** -0.5, 0.375)
    proj_second = gaussian(key_list[7], (C, C), C ** -0.5, 0.375)
    gain_first = jnp.clip(1.0 + 0.16 * jax.random.normal(key_list[8], (C,), jnp.float32), 0.2, 1.8)
    gain_second = jnp.clip(1.0 + 0.16 * jax.random.normal(key_list[9], (C,), jnp.float32), 0.2, 1.8)
    return dict(inputs=inputs, cotangent=cotangent, taps_first=taps_first, taps_second=taps_second, bias_first=bias_first, bias_second=bias_second, proj_first=proj_first, proj_second=proj_second, gain_first=gain_first, gain_second=gain_second)


gelu_coef = 0.7978845608028654

def gelu_tanh(values):
    inner = jnp.tanh(gelu_coef * (values + 0.044715 * values * values * values))
    return 0.5 * values * (1.0 + inner)

def gelu_slope(values):
    inner = jnp.tanh(gelu_coef * (values + 0.044715 * values * values * values))
    return 0.5 * (1.0 + inner) + 0.5 * values * (1.0 - inner * inner) * gelu_coef * (1.0 + 3.0 * 0.044715 * values * values)

def matmul(left, right):
    return jnp.dot(left, right, preferred_element_type=jnp.float32)

def row_product(left, right):
    left_rows = left.reshape(-1, left.shape[-1])
    right_rows = right.reshape(-1, right.shape[-1])
    return lax.dot_general(left_rows, right_rows, (((0,), (0,)), ((), ())), preferred_element_type=jnp.float32)

def full_move(values, offset):
    distance = abs(offset) * POS_DEV
    filler = jnp.zeros((values.shape[0], distance, values.shape[2]), values.dtype)
    if offset > 0:
        return jnp.concatenate([filler, values[:, :values.shape[1] - distance]], axis=1)
    return jnp.concatenate([values[:, distance:], filler], axis=1)

def norm_input(source, gain_vec):
    x_wide = source.astype(jnp.float32)
    inv_rms = lax.rsqrt(lax.optimization_barrier(jnp.mean(x_wide * x_wide, axis=-1, keepdims=True)) + 1e-06)
    return (x_wide, inv_rms, x_wide * inv_rms * gain_vec)

def layer_forward(source, params, move):
    kernel, bias_vec, project, gain_vec, jumps = params
    x_wide, inv_rms, normed = norm_input(source, gain_vec)
    activations = gelu_tanh(normed).astype(jnp.bfloat16)
    earlier = move(activations, jumps)
    ahead = move(activations, -jumps)
    hidden = matmul(earlier, kernel[0]) + matmul(activations, kernel[1]) + matmul(ahead, kernel[2]) + bias_vec
    gelled = gelu_tanh(hidden).astype(jnp.bfloat16)
    result = (x_wide + matmul(gelled, project)).astype(jnp.bfloat16)
    return (result, (activations, earlier, ahead, hidden, gelled))

def layer_backward(source, grad_out, params, stored, move):
    kernel, bias_vec, project, gain_vec, jumps = params
    activations, earlier, ahead, hidden, gelled = stored
    proj_grad = row_product(gelled, grad_out)
    grad_hidden = (matmul(grad_out, project.T) * gelu_slope(hidden)).astype(jnp.bfloat16)
    tap_grad = jnp.stack([row_product(earlier, grad_hidden), row_product(activations, grad_hidden), row_product(ahead, grad_hidden)])
    from_ahead = move(grad_hidden, -jumps)
    from_behind = move(grad_hidden, jumps)
    grad_acts = matmul(grad_hidden, kernel[1].T) + matmul(from_ahead, kernel[0].T) + matmul(from_behind, kernel[2].T)
    x_wide, inv_rms, normed = norm_input(source, gain_vec)
    weighted = grad_acts * gelu_slope(normed) * gain_vec
    grad_in = grad_out.astype(jnp.float32) + inv_rms * weighted - x_wide * inv_rms * inv_rms * inv_rms * lax.optimization_barrier(jnp.mean(x_wide * weighted, axis=-1, keepdims=True))
    return (grad_in.astype(jnp.bfloat16), tap_grad, proj_grad)

def reference(inputs, cotangent, taps_first, taps_second, bias_first, bias_second, proj_first, proj_second, gain_first, gain_second):
    first = (taps_first, bias_first, proj_first, gain_first, HOP1)
    second = (taps_second, bias_second, proj_second, gain_second, HOP2)
    middle, stored_first = layer_forward(inputs, first, full_move)
    outputs, stored_second = layer_forward(middle, second, full_move)
    middle_grad, taps_two, proj_two = layer_backward(middle, cotangent, second, stored_second, full_move)
    input_grad, taps_one, proj_one = layer_backward(inputs, middle_grad, first, stored_first, full_move)
    weight_scale = 1.0 / jnp.sqrt(jnp.float32(WINDOWS * LEN))
    return (outputs, input_grad, taps_one * weight_scale, taps_two * weight_scale, proj_one * weight_scale, proj_two * weight_scale)
```

```python
import functools
import math

import jax
import jax.numpy as jnp
from jax import lax
from jax.experimental import pallas as pl
from jax.experimental.pallas import tpu as pltpu
from jax.sharding import Mesh
from jax.sharding import PartitionSpec as P

HOP1 = 4
HOP2 = 8

GELU_COEF = 0.7978845608028654
CUBIC = 0.044715
BF16 = jnp.bfloat16
F32 = jnp.float32


def gelu_parts(v):
    square = v * v
    th = jnp.tanh(v * (GELU_COEF + (GELU_COEF * CUBIC) * square))
    half = 0.5 + 0.5 * th
    value = v * half
    slope = half + value * (1.0 - th) * (GELU_COEF + (3.0 * CUBIC * GELU_COEF) * square)
    return value, slope


def inverse_rms(x):
    return lax.rsqrt(jnp.mean(x * x, axis=-1, keepdims=True) + 1e-06)


def dot(left, right):
    return jnp.dot(left, right, preferred_element_type=F32)


def row_dot(left, right):
    return lax.dot_general(left, right, (((0,), (0,)), ((), ())), preferred_element_type=F32)


def conv_at(parts, taps, p, hop):
    n, width = len(parts), parts[0].shape[-1]
    low = 0 if p - hop >= 0 else 1
    high = 3 if p + hop < n else 2
    left = jnp.concatenate([parts[p + (k - 1) * hop] for k in range(low, high)], axis=-1)
    return dot(left, taps[low * width : high * width, :])


def forward_kernel(hops, x_ref, *refs):
    weights, outs = refs[:8], refs[8:]
    n, tile, width = x_ref.shape
    source = [x_ref[p].astype(F32) for p in range(n)]
    for block in range(2):
        taps, bias, project, gain = weights[4 * block : 4 * block + 4]
        act_out, norm_slope_out, gelled_out, hidden_slope_out, result_out = outs[
            5 * block : 5 * block + 5
        ]
        gain_row = gain[...]
        acts = []
        for p in range(n):
            normed = source[p] * inverse_rms(source[p]) * gain_row
            value, slope = gelu_parts(normed)
            act = value.astype(BF16)
            acts.append(act)
            act_out[p] = act
            norm_slope_out[p] = (slope * gain_row).astype(BF16)
        results = []
        for p in range(n):
            hidden = conv_at(acts, taps, p, hops[block]) + bias[...]
            value, slope = gelu_parts(hidden)
            gelled = value.astype(BF16)
            gelled_out[p] = gelled
            hidden_slope_out[p] = slope.astype(BF16)
            result = (source[p] + dot(gelled, project[...])).astype(BF16)
            result_out[p] = result
            results.append(result.astype(F32))
        source = results


def backward_kernel(hops, y_ref, *refs):
    stored, weights = refs[:10], refs[10:14]
    grad_in_out, grads_out = refs[14], refs[15]
    sums = refs[16]
    n, tile, width = y_ref.shape

    @pl.when(pl.program_id(0) == 0)
    def _():
        sums[...] = jnp.zeros_like(sums)

    grads = [y_ref[p] for p in range(n)]
    for block in (1, 0):
        source, act, norm_slope, gelled, hidden_slope = stored[5 * block : 5 * block + 5]
        taps_t, project_t = weights[2 * block : 2 * block + 2]
        hop = hops[block]
        hidden_grads = []
        for p in range(n):
            hidden = dot(grads[p], project_t[...]) * hidden_slope[p].astype(F32)
            hidden_grads.append(hidden.astype(BF16))
        proj_sum = row_dot(gelled[...].reshape(n * tile, width), jnp.concatenate(grads, axis=0))
        sums[4 * block + 3] += proj_sum
        stacked = jnp.concatenate(hidden_grads, axis=0)
        flat = act[...].reshape(n * tile, width)
        cut = hop * tile
        sums[4 * block] += row_dot(flat[: n * tile - cut], stacked[cut:])
        sums[4 * block + 1] += row_dot(flat, stacked)
        sums[4 * block + 2] += row_dot(flat[cut:], stacked[: n * tile - cut])
        for p in range(n):
            weighted = conv_at(hidden_grads, taps_t, p, hop) * norm_slope[p].astype(F32)
            x = source[p].astype(F32)
            inv = inverse_rms(x)
            unit = x * inv
            mean = jnp.mean(unit * weighted, axis=-1, keepdims=True)
            grads[p] = (grads[p].astype(F32) + inv * (weighted - unit * mean)).astype(BF16)
    for p in range(n):
        grad_in_out[p] = grads[p]

    @pl.when(pl.program_id(0) == pl.num_programs(0) - 1)
    def _():
        grads_out[...] = sums[...].astype(BF16)


def tile_of(n, rows):
    tile = max(16, 512 // n)
    while rows % tile:
        tile //= 2
    return tile


def whole(array):
    zeros = (0,) * array.ndim
    return pl.BlockSpec(array.shape, lambda i: zeros)


def run_forward(x, weights, hops):
    n, rows, width = x.shape
    tile = tile_of(n, rows)
    spec = pl.BlockSpec((n, tile, width), lambda i: (0, i, 0))
    return pl.pallas_call(
        functools.partial(forward_kernel, hops),
        name="forward",
        grid=(rows // tile,),
        in_specs=[spec] + [whole(w) for w in weights],
        out_specs=[spec] * 10,
        out_shape=[jax.ShapeDtypeStruct(x.shape, BF16)] * 10,
        compiler_params=pltpu.CompilerParams(vmem_limit_bytes=48 << 20),
        cost_estimate=pl.CostEstimate(
            flops=16 * x.size * width, bytes_accessed=22 * x.size, transcendentals=4 * x.size
        ),
    )(x, *weights)


def run_backward(y, stored, weights, hops):
    n, rows, width = y.shape
    tile = tile_of(n, rows)
    spec = pl.BlockSpec((n, tile, width), lambda i: (0, i, 0))
    sums = jax.ShapeDtypeStruct((8, width, width), BF16)
    return pl.pallas_call(
        functools.partial(backward_kernel, hops),
        name="backward",
        grid=(rows // tile,),
        in_specs=[spec] * 11 + [whole(w) for w in weights],
        out_specs=[spec, whole(sums)],
        out_shape=[jax.ShapeDtypeStruct(y.shape, BF16), sums],
        scratch_shapes=[pltpu.VMEM((8, width, width), F32)],
        compiler_params=pltpu.CompilerParams(vmem_limit_bytes=48 << 20),
        cost_estimate=pl.CostEstimate(
            flops=32 * y.size * width, bytes_accessed=24 * y.size, transcendentals=0
        ),
    )(y, *stored, *weights)


def exchange(blocks):
    return lax.all_to_all(blocks, "chain", 0, 0, tiled=True)


def reduce_over(values, axis):
    size = lax.axis_size(axis)
    parts = values.reshape((size, values.shape[0] // size) + values.shape[1:])
    parts = lax.all_to_all(parts, axis, 0, 0, tiled=True)
    return parts.astype(F32).sum(0).astype(BF16)


def on_device(
    inputs,
    cotangent,
    taps_first,
    taps_second,
    bias_first,
    bias_second,
    proj_first,
    proj_second,
    gain_first,
    gain_second,
):
    n = lax.axis_size("chain")
    hops = (1, HOP2 // HOP1)
    shape = inputs.shape
    width = shape[-1]
    blocks = (n, shape[0] * shape[1] // n, width)
    weight_scale = 1.0 / math.sqrt(shape[0] * shape[1] * n * HOP1)

    x = exchange(inputs.reshape(blocks))
    y = exchange(cotangent.reshape(blocks))
    flat = (3 * width, width)
    forward_weights = (
        taps_first.reshape(flat), bias_first[None], proj_first, gain_first[None],
        taps_second.reshape(flat), bias_second[None], proj_second, gain_second[None],
    )
    backward_weights = (
        taps_first[::-1].transpose(0, 2, 1).reshape(flat), proj_first.T,
        taps_second[::-1].transpose(0, 2, 1).reshape(flat), proj_second.T,
    )
    act1, norm1, gelled1, hidden1, middle, act2, norm2, gelled2, hidden2, result = run_forward(
        x, forward_weights, hops
    )
    result = exchange(result).reshape(shape)
    stored = (x, act1, norm1, gelled1, hidden1, middle, act2, norm2, gelled2, hidden2)
    grad_in, grads = run_backward(y, stored, backward_weights, hops)
    grad_in = exchange(grad_in).reshape(shape)

    grads = reduce_over(grads.reshape(8 * width, width), "lane")
    grads = reduce_over(grads, "chain")
    grads = lax.all_gather(grads, "chain", axis=0, tiled=True)
    grads = lax.all_gather(grads, "lane", axis=0, tiled=True)
    grads = grads.reshape(2, 4, width, width).astype(F32) * weight_scale
    return (result, grad_in, grads[0, :3], grads[1, :3], grads[0, 3], grads[1, 3])


def solution(mesh):
    groups, seq = mesh.shape["groups"], mesh.shape["seq"]
    own = Mesh(
        mesh.devices.reshape(groups, seq // HOP1, HOP1), ("groups", "chain", "lane")
    )
    split = P("groups", ("chain", "lane"), None)
    return jax.shard_map(
        on_device,
        mesh=own,
        in_specs=(split, split) + (P(),) * 8,
        out_specs=(
            split,
            split,
            P("groups", None, None),
            P("groups", None, None),
            P("groups", None),
            P("groups", None),
        ),
        check_vma=False,
    )
```

```python
import functools
import math

import jax
import jax.numpy as jnp
from jax import lax
from jax.experimental import pallas as pl
from jax.experimental.pallas import tpu as pltpu
from jax.sharding import Mesh
from jax.sharding import PartitionSpec as P

HOP1 = 4
HOP2 = 8

GELU_COEF = 0.7978845608028654
CUBIC = 0.044715
CHUNKS = 2
FLOPS = 1000
VMEM_LIMIT = 60 << 20
BF16 = jnp.bfloat16
F32 = jnp.float32


def gelu_parts(v):
    square = v * v
    th = jnp.tanh(v * (GELU_COEF + (GELU_COEF * CUBIC) * square))
    half = 0.5 + 0.5 * th
    value = v * half
    slope = half + value * (1.0 - th) * (GELU_COEF + (3.0 * CUBIC * GELU_COEF) * square)
    return value, slope


def inverse_rms(x):
    return lax.rsqrt(jnp.mean(x * x, axis=-1, keepdims=True) + 1e-06)


def dot(left, right):
    return jnp.dot(left, right, preferred_element_type=F32)


def row_dot(left, right):
    return lax.dot_general(left, right, (((0,), (0,)), ((), ())), preferred_element_type=F32)


def conv_at(parts, tile, taps, p, n, hop):
    width = parts.shape[-1]
    low = 0 if p - hop >= 0 else 1
    high = 3 if p + hop < n else 2
    left = jnp.concatenate(
        [parts[pl.ds((p + (k - 1) * hop) * tile, tile), :] for k in range(low, high)], axis=-1
    )
    return dot(left, taps[low * width : high * width, :])


def over_rows(total, body, step=64):
    def one(i, carry):
        body(pl.ds(pl.multiple_of(i * step, step), step))
        return carry

    lax.fori_loop(0, total // step, one, 0, unroll=2)


def chunk_kernel(n, hops, last, me_ref, *refs):
    own_ref, pieces, weights = refs[0], refs[1:n], refs[n : n + 12]
    refs = refs[n + 12 :]
    if last:
        before, refs = refs[0], refs[1:]
    own_out, piece_outs, refs = refs[0], refs[1:n], refs[n:]
    if last:
        keep_out, send_out, sums = refs[:3]
        refs = refs[3:]
    else:
        sums, refs = refs[0], refs[1:]
    sources, grad, wide, hidden_grad, acts, gelleds, norm_slopes, hidden_slopes = refs
    me, core = me_ref[0], me_ref[1]
    tile, width = own_ref.shape[1:]
    total = n * tile

    for s in range(n):
        piece = own_ref if s == 0 else pieces[s - 1]
        rows = pl.ds(pl.multiple_of((me ^ s) * tile, tile), tile)
        sources[0, rows, :] = piece[0]
        grad[rows, :] = piece[1]

    for block in range(2):
        taps, bias, project, gain = weights[4 * block : 4 * block + 4]
        gain_row, bias_row = gain[...], bias[...]

        def before_conv(rows):
            x = sources[block, rows, :].astype(F32)
            value, slope = gelu_parts(x * inverse_rms(x) * gain_row)
            acts[block, rows, :] = value.astype(BF16)
            norm_slopes[block, rows, :] = slope * gain_row

        over_rows(total, before_conv)
        for p in range(n):
            wide[pl.ds(p * tile, tile), :] = conv_at(
                acts.at[block], tile, taps, p, n, hops[block]
            )

        def after_conv(rows):
            value, slope = gelu_parts(wide[rows, :] + bias_row)
            gelleds[block, rows, :] = value.astype(BF16)
            hidden_slopes[block, rows, :] = slope

        over_rows(total, after_conv)
        sources[block + 1] = (
            sources[block].astype(F32) + dot(gelleds[block], project[...])
        ).astype(BF16)

    def send(source, k):
        for s in range(n):
            piece = own_out if s == 0 else piece_outs[s - 1]
            piece[k] = source[pl.ds(pl.multiple_of((me ^ s) * tile, tile), tile), :]

    send(sources.at[2], 0)

    def add(k, value):
        sums[k] = before[k] + value if last else value

    for block in (1, 0):
        taps_t, project_t = weights[8 + 2 * block : 10 + 2 * block]
        hop = hops[block]
        cut = hop * tile
        add(4 * block + 3, row_dot(gelleds[block], grad[...]))
        wide[...] = dot(grad[...], project_t[...])

        def hidden_rows(rows):
            hidden_grad[rows, :] = (wide[rows, :] * hidden_slopes[block, rows, :]).astype(BF16)

        over_rows(total, hidden_rows)
        add(4 * block, row_dot(acts[block, : total - cut, :], hidden_grad[cut:, :]))
        add(4 * block + 1, row_dot(acts[block], hidden_grad[...]))
        add(4 * block + 2, row_dot(acts[block, cut:, :], hidden_grad[: total - cut, :]))
        for p in range(n):
            wide[pl.ds(p * tile, tile), :] = conv_at(hidden_grad, tile, taps_t, p, n, hop)

        def source_rows(rows):
            weighted = wide[rows, :] * norm_slopes[block, rows, :]
            x = sources[block, rows, :].astype(F32)
            inv = inverse_rms(x)
            unit = x * inv
            mean = jnp.mean(unit * weighted, axis=-1, keepdims=True)
            grad[rows, :] = (
                grad[rows, :].astype(F32) + inv * (weighted - unit * mean)
            ).astype(BF16)

        over_rows(total, source_rows)

    send(grad, 1)
    if last:
        keep_out[...] = sums[pl.ds(4 * core, 4)]
        send_out[...] = sums[pl.ds(4 * (1 - core), 4)].astype(BF16)


def run_chunk(me, pieces, weights, before, hops):
    n, (_, rows, width) = len(pieces), pieces[0].shape
    last = before is not None
    total = n * rows
    full = jax.ShapeDtypeStruct((8, width, width), F32)
    half = (4, width, width)
    sums = [jax.ShapeDtypeStruct(half, F32), jax.ShapeDtypeStruct(half, BF16)]
    scratch = [pltpu.VMEM(full.shape, F32)] if last else []
    operands = [*pieces, *weights] + ([before] if last else [])
    outs = pl.pallas_call(
        functools.partial(chunk_kernel, n, hops, last),
        name="chunk",
        in_specs=[pl.BlockSpec(memory_space=pltpu.SMEM)]
        + [pl.BlockSpec(operand.shape, None) for operand in operands],
        out_shape=[jax.ShapeDtypeStruct(pieces[0].shape, BF16)] * n + (sums if last else [full]),
        scratch_shapes=scratch
        + [
            pltpu.VMEM((3, total, width), BF16),
            pltpu.VMEM((total, width), BF16),
            pltpu.VMEM((total, width), F32),
            pltpu.VMEM((total, width), BF16),
            pltpu.VMEM((2, total, width), BF16),
            pltpu.VMEM((2, total, width), BF16),
            pltpu.VMEM((2, total, width), F32),
            pltpu.VMEM((2, total, width), F32),
        ],
        compiler_params=pltpu.CompilerParams(vmem_limit_bytes=VMEM_LIMIT),
        cost_estimate=pl.CostEstimate(flops=FLOPS, bytes_accessed=FLOPS, transcendentals=0),
    )(me, *operands)
    return list(outs[:n]), list(outs[n:])


def take(array, index):
    return lax.dynamic_index_in_dim(array, index, 0, keepdims=False)


def swap(values, axis, s=1):
    return lax.ppermute(values, axis, [(i, i ^ s) for i in range(lax.axis_size(axis))])


def spread(array, me):
    n = array.shape[0]
    return [swap(take(array, me ^ s), "chain", s) for s in range(1, n)]


def assemble(pieces, me):
    out = jnp.stack(pieces)
    return jnp.take(out, me ^ jnp.arange(len(pieces)), axis=0)


def on_device(
    inputs,
    cotangent,
    taps_first,
    taps_second,
    bias_first,
    bias_second,
    proj_first,
    proj_second,
    gain_first,
    gain_second,
):
    n = lax.axis_size("chain")
    place, pair, core = (lax.axis_index(axis) for axis in ("chain", "pair", "core"))
    me = jnp.stack([place, core]).astype(jnp.int32)
    hops = (1, HOP2 // HOP1)
    shape = inputs.shape
    width = shape[-1]
    weight_scale = 1.0 / math.sqrt(shape[0] * shape[1] * n * HOP1)
    rows = shape[0] * shape[1] // (CHUNKS * n)
    both = jnp.stack([inputs, cotangent]).reshape(2, CHUNKS, n, rows, width)

    def block_of(chunk, s):
        start = (0, chunk, place ^ s, 0, 0)
        return lax.dynamic_slice(both, start, (2, 1, 1, rows, width)).reshape(2, rows, width)

    flat = (3 * width, width)
    weights = (
        taps_first.reshape(flat), bias_first[None], proj_first, gain_first[None],
        taps_second.reshape(flat), bias_second[None], proj_second, gain_second[None],
        taps_first[::-1].transpose(0, 2, 1).reshape(flat), proj_first.T,
        taps_second[::-1].transpose(0, 2, 1).reshape(flat), proj_second.T,
    )
    order = sorted(range(1, n), reverse=True)
    arrived = [{}, {}]
    for s in order:
        arrived[0][s] = swap(block_of(0, s), "chain", s)
    for s in order:
        arrived[0][s], block = lax.optimization_barrier((arrived[0][s], block_of(1, s)))
        arrived[1][s] = swap(block, "chain", s)

    def pieces_of(chunk):
        return [block_of(chunk, 0)] + [arrived[chunk][s] for s in range(1, n)]

    def send_back(pieces):
        return pieces[:1] + [swap(pieces[s], "chain", s) for s in range(1, n)]

    results = [None, None]
    pieces, before = run_chunk(me, pieces_of(0), weights, None, hops)
    pieces, last_pieces = lax.optimization_barrier((pieces, pieces_of(1)))
    results[0] = send_back(pieces)
    pieces, (keep, send) = run_chunk(me, last_pieces, weights, before[0], hops)
    results[1] = send_back(pieces)

    results[0][3], send = lax.optimization_barrier((results[0][3], send))
    got = swap(send, "core")
    half = (keep + got).reshape(2, 2 * width, width)
    got = swap(take(half, 1 - pair).astype(BF16), "pair")
    quarter = (take(half, pair) + got).reshape(n, 2 * width // n, width)
    results[0], quarter = lax.optimization_barrier((results[0], quarter))
    got = spread(quarter.astype(BF16), place)
    total = take(quarter, place)
    for part in got:
        total = total + part
    total = (total * weight_scale).astype(BF16)

    quarter = assemble([total] + [swap(total, "chain", s) for s in range(1, n)], place)
    results[1][3], quarter = lax.optimization_barrier((results[1][3], quarter))
    quarter = quarter.reshape(2 * width, width)
    half = jnp.stack([quarter, swap(quarter, "pair")])
    half = jnp.where(pair == 0, half, half[::-1]).reshape(4, width, width)
    other = swap(half, "core")
    first = jnp.where(core == 0, half, other).astype(F32)
    second = jnp.where(core == 0, other, half).astype(F32)
    outputs = jnp.stack([assemble(pieces, place) for pieces in results])
    return (
        outputs[:, :, 0].reshape(shape),
        outputs[:, :, 1].reshape(shape),
        first[:3],
        second[:3],
        first[3],
        second[3],
    )


def solution(mesh):
    groups, seq = mesh.shape["groups"], mesh.shape["seq"]
    own = Mesh(
        mesh.devices.reshape(groups, seq // HOP1, HOP1 // 2, 2),
        ("groups", "chain", "pair", "core"),
    )
    split = P("groups", ("chain", "pair", "core"), None)
    return jax.shard_map(
        on_device,
        mesh=own,
        in_specs=(split, split) + (P(),) * 8,
        out_specs=(
            split,
            split,
            P("groups", None, None),
            P("groups", None, None),
            P("groups", None),
            P("groups", None),
        ),
        check_vma=False,
    )
```

```python
import functools
import math

import jax
import jax.numpy as jnp
from jax import lax
from jax.experimental import pallas as pl
from jax.experimental.pallas import tpu as pltpu
from jax.sharding import Mesh
from jax.sharding import PartitionSpec as P

HOP1 = 4
HOP2 = 8

GELU_COEF = 0.7978845608028654
CUBIC = 0.044715
CHUNKS = 2
VMEM_LIMIT = 60 << 20
BF16 = jnp.bfloat16
F32 = jnp.float32


def gelu_parts(v):
    square = v * v
    th = jnp.tanh(v * (GELU_COEF + (GELU_COEF * CUBIC) * square))
    half = 0.5 + 0.5 * th
    value = v * half
    slope = half + value * (1.0 - th) * (GELU_COEF + (3.0 * CUBIC * GELU_COEF) * square)
    return value, slope


def inverse_rms(x):
    return lax.rsqrt(jnp.mean(x * x, axis=-1, keepdims=True) + 1e-06)


def dot(left, right):
    return jnp.dot(left, right, preferred_element_type=F32)


def row_dot(left, right):
    return lax.dot_general(left, right, (((0,), (0,)), ((), ())), preferred_element_type=F32)


def conv_at(parts, tile, taps, p, n, hop):
    width = parts.shape[-1]
    low = 0 if p - hop >= 0 else 1
    high = 3 if p + hop < n else 2
    left = jnp.concatenate(
        [parts[pl.ds((p + (k - 1) * hop) * tile, tile), :] for k in range(low, high)], axis=-1
    )
    return dot(left, taps[low * width : high * width, :])


def over_rows(total, body, step=64):
    for start in range(0, total, step):
        body(pl.ds(start, step))


def start_all(copies):
    for copy in copies:
        copy.start()
    return copies


def wait_all(copies):
    for copy in copies:
        copy.wait()


def stage(moves, held, sems):
    into, out = [], []
    for i, (source, target) in enumerate(moves):
        into.append(pltpu.make_async_copy(source, held.at[i], sems.at[0, i]))
        out.append(pltpu.make_async_copy(held.at[i], target, sems.at[1, i]))
    start_all(into)
    for arrival, departure in zip(into, out):
        arrival.wait()
        departure.start()
    wait_all(out)


def pick_kernel(n, chunk, inputs, cotangent, *refs):
    pieces, (held, sems) = refs[:-2], refs[-2:]
    me = lax.axis_index("chain")
    moves = [
        (source.at[chunk * n + (me ^ s)], pieces[s - 1].at[k])
        for s in reversed(range(1, n))
        for k, source in enumerate((inputs, cotangent))
    ]
    stage(moves, held, sems)


def pick(inputs, cotangent, n, chunk):
    _, rows, width = inputs.shape
    piece = jax.ShapeDtypeStruct((2, rows, width), BF16)
    return pl.pallas_call(
        functools.partial(pick_kernel, n, chunk),
        name="pick",
        in_specs=in_place(2),
        out_specs=in_place(n - 1),
        out_shape=[piece] * (n - 1),
        scratch_shapes=[
            pltpu.VMEM((2 * (n - 1), rows, width), BF16),
            pltpu.SemaphoreType.DMA((2, 2 * (n - 1))),
        ],
        cost_estimate=small_cost(),
    )(inputs, cotangent)


def put_kernel(n, chunk, fresh, *refs):
    pieces, refs = refs[:n], refs[n if fresh else n + 2 :]
    outs, (held, sems) = refs[:2], refs[2:]
    me = lax.axis_index("chain")
    moves = [
        (pieces[s].at[k], outs[k].at[chunk * n + (me ^ s)]) for s in range(n) for k in range(2)
    ]
    stage(moves, held, sems)


def put(pieces, chunk, into):
    n, (_, rows, width) = len(pieces), pieces[0].shape
    full = jax.ShapeDtypeStruct((CHUNKS * n, rows, width), BF16)
    return pl.pallas_call(
        functools.partial(put_kernel, n, chunk, into is None),
        name="put",
        in_specs=in_place(n if into is None else n + 2),
        out_specs=in_place(2),
        out_shape=[full, full],
        input_output_aliases={} if into is None else {n: 0, n + 1: 1},
        scratch_shapes=[
            pltpu.VMEM((2 * n, rows, width), BF16),
            pltpu.SemaphoreType.DMA((2, 2 * n)),
        ],
        cost_estimate=pl.CostEstimate(
            flops=0, bytes_accessed=16 * n * rows * width, transcendentals=0
        ),
    )(*pieces, *(into or ()))


def finish_kernel(own, by_pair, by_core, by_both, *refs):
    outs, held, sems = refs[:4], refs[4], refs[5]
    pair, core = lax.axis_index("pair"), lax.axis_index("core")
    places = ((core, pair), (core, 1 - pair), (1 - core, pair), (1 - core, 1 - pair))
    wait_all(
        start_all(
            [
                pltpu.make_async_copy(quarter, held.at[block, half], sems.at[i])
                for i, (quarter, (block, half)) in enumerate(
                    zip((own, by_pair, by_core, by_both), places)
                )
            ]
        )
    )
    for block in range(2):
        taps, project = outs[block], outs[2 + block]
        taps[0] = held[block, 0, 0].astype(F32)
        taps[1] = held[block, 0, 1].astype(F32)
        taps[2] = held[block, 1, 0].astype(F32)
        project[...] = held[block, 1, 1].astype(F32)


def finish(quarters, width):
    quarters = [quarter.reshape(2, width, width) for quarter in quarters]
    taps = jax.ShapeDtypeStruct((3, width, width), F32)
    project = jax.ShapeDtypeStruct((width, width), F32)
    return pl.pallas_call(
        finish_kernel,
        name="finish",
        in_specs=in_place(4),
        out_shape=[taps, taps, project, project],
        scratch_shapes=[
            pltpu.VMEM((2, 2, 2, width, width), BF16),
            pltpu.SemaphoreType.DMA((4,)),
        ],
        compiler_params=pltpu.CompilerParams(vmem_limit_bytes=VMEM_LIMIT),
        cost_estimate=small_cost(),
    )(*quarters)


def in_place(count):
    return [pl.BlockSpec(memory_space=pl.ANY)] * count


def small_cost():
    return pl.CostEstimate(flops=1000, bytes_accessed=1000, transcendentals=0)


def chunk_kernel(n, hops, chunk, last, *refs):
    inputs, cotangent, refs = refs[0], refs[1], refs[2:]
    pieces, weights, late, refs = refs[: n - 1], refs[n - 1 : n + 7], refs[n + 7 : n + 11], refs[n + 11 :]
    if last:
        before, refs = refs[0], refs[1:]
    piece_outs, refs = refs[:n], refs[n:]
    if last:
        keep_out, send_out, sums = refs[:3]
        refs = refs[3:]
    else:
        sums, refs = refs[0], refs[1:]
    sources, grad, wide, hidden_grad, acts, gelleds, norm_slopes, hidden_slopes = refs[:8]
    late_held, sems, late_sems = refs[8:12], refs[12], refs[13]
    me, core = lax.axis_index("chain"), lax.axis_index("core")
    _, rows_in, width = inputs.shape
    tile, total = rows_in, n * rows_in

    def place(s):
        return pl.ds(pl.multiple_of((me ^ s) * tile, tile), tile)

    def arriving(k, held, whole_array):
        copies = []
        for s in range(n):
            source = whole_array.at[chunk * n + me] if s == 0 else pieces[s - 1].at[k]
            copies.append(pltpu.make_async_copy(source, held.at[place(s), :], sems.at[k, s]))
        return start_all(copies)

    def leaving(k, held):
        copies = []
        for s in range(n):
            copies.append(
                pltpu.make_async_copy(
                    held.at[place(s), :], piece_outs[s].at[k], sems.at[2 + k, s]
                )
            )
        return start_all(copies)

    x_copies = arriving(0, sources.at[0], inputs)
    late_copies = start_all(
        [
            pltpu.make_async_copy(source, held, late_sems.at[i])
            for i, (source, held) in enumerate(zip(late, late_held))
        ]
    )
    y_copies = arriving(1, grad, cotangent)
    if last:
        late_copies += start_all([pltpu.make_async_copy(before, sums, late_sems.at[4])])
    wait_all(x_copies)

    for block in range(2):
        taps, bias, project, gain = weights[4 * block : 4 * block + 4]
        gain_row, bias_row = gain[...], bias[...]

        def before_conv(rows):
            x = sources[block, rows, :].astype(F32)
            value, slope = gelu_parts(x * inverse_rms(x) * gain_row)
            acts[block, rows, :] = value.astype(BF16)
            norm_slopes[block, rows, :] = slope * gain_row

        over_rows(total, before_conv)
        for p in range(n):
            wide[pl.ds(p * tile, tile), :] = conv_at(
                acts.at[block], tile, taps, p, n, hops[block]
            )

        def after_conv(rows):
            value, slope = gelu_parts(wide[rows, :] + bias_row)
            gelleds[block, rows, :] = value.astype(BF16)
            hidden_slopes[block, rows, :] = slope

        over_rows(total, after_conv)
        sources[block + 1] = (
            sources[block].astype(F32) + dot(gelleds[block], project[...])
        ).astype(BF16)

    out_copies = leaving(0, sources.at[2])
    wait_all(y_copies + late_copies)

    def add(k, value):
        sums[k] = sums[k] + value if last else value

    for block in (1, 0):
        taps_t, project_t = late_held[2 * block : 2 * block + 2]
        hop = hops[block]
        cut = hop * tile
        add(4 * block + 3, row_dot(gelleds[block], grad[...]))
        wide[...] = dot(grad[...], project_t[...])

        def hidden_rows(rows):
            hidden_grad[rows, :] = (wide[rows, :] * hidden_slopes[block, rows, :]).astype(BF16)

        over_rows(total, hidden_rows)
        add(4 * block, row_dot(acts[block, : total - cut, :], hidden_grad[cut:, :]))
        add(4 * block + 1, row_dot(acts[block], hidden_grad[...]))
        add(4 * block + 2, row_dot(acts[block, cut:, :], hidden_grad[: total - cut, :]))
        for p in range(n):
            wide[pl.ds(p * tile, tile), :] = conv_at(hidden_grad, tile, taps_t, p, n, hop)

        def source_rows(rows):
            weighted = wide[rows, :] * norm_slopes[block, rows, :]
            x = sources[block, rows, :].astype(F32)
            inv = inverse_rms(x)
            unit = x * inv
            mean = jnp.mean(unit * weighted, axis=-1, keepdims=True)
            grad[rows, :] = (
                grad[rows, :].astype(F32) + inv * (weighted - unit * mean)
            ).astype(BF16)

        over_rows(total, source_rows)

    out_copies += leaving(1, grad)
    if last:
        keep_out[...] = sums[pl.ds(4 * core, 4)]
        send_out[...] = sums[pl.ds(4 * (1 - core), 4)].astype(BF16)
    wait_all(out_copies)


def run_chunk(inputs, cotangent, pieces, weights, late, before, hops, chunk):
    n, (_, rows, width) = len(pieces) + 1, pieces[0].shape
    last = before is not None
    total = n * rows
    full = jax.ShapeDtypeStruct((8, width, width), F32)
    half = (4, width, width)
    sums = [jax.ShapeDtypeStruct(half, F32), jax.ShapeDtypeStruct(half, BF16)] if last else [full]
    operands = [inputs, cotangent, *pieces, *weights, *late] + ([before] if last else [])
    scratch = [pltpu.VMEM(full.shape, F32)] if last else []
    outs = pl.pallas_call(
        functools.partial(chunk_kernel, n, hops, chunk, last),
        name="chunk",
        in_specs=in_place(n + 1)
        + [pl.BlockSpec(weight.shape, None) for weight in weights]
        + in_place(5 if last else 4),
        out_specs=in_place(n) + [pl.BlockSpec(kind.shape, None) for kind in sums],
        out_shape=[jax.ShapeDtypeStruct(pieces[0].shape, BF16)] * n + sums,
        scratch_shapes=scratch
        + [
            pltpu.VMEM((3, total, width), BF16),
            pltpu.VMEM((total, width), BF16),
            pltpu.VMEM((total, width), F32),
            pltpu.VMEM((total, width), BF16),
            pltpu.VMEM((2, total, width), BF16),
            pltpu.VMEM((2, total, width), BF16),
            pltpu.VMEM((2, total, width), F32),
            pltpu.VMEM((2, total, width), F32),
        ]
        + [pltpu.VMEM(weight.shape, BF16) for weight in late]
        + [pltpu.SemaphoreType.DMA((4, n)), pltpu.SemaphoreType.DMA((5,))],
        compiler_params=pltpu.CompilerParams(vmem_limit_bytes=VMEM_LIMIT),
        cost_estimate=small_cost(),
    )(*operands)
    return list(outs[:n]), list(outs[n:])


def take(array, index):
    return lax.dynamic_index_in_dim(array, index, 0, keepdims=False)


def swap(values, axis, s=1):
    return lax.ppermute(values, axis, [(i, i ^ s) for i in range(lax.axis_size(axis))])


def spread(array, me):
    n = array.shape[0]
    return [swap(take(array, me ^ s), "chain", s) for s in range(1, n)]


def assemble(pieces, me):
    out = jnp.stack(pieces)
    return jnp.take(out, me ^ jnp.arange(len(pieces)), axis=0)


def on_device(
    inputs,
    cotangent,
    taps_first,
    taps_second,
    bias_first,
    bias_second,
    proj_first,
    proj_second,
    gain_first,
    gain_second,
):
    n = lax.axis_size("chain")
    place, pair = lax.axis_index("chain"), lax.axis_index("pair")
    hops = (1, HOP2 // HOP1)
    shape = inputs.shape
    width = shape[-1]
    weight_scale = 1.0 / math.sqrt(shape[0] * shape[1] * n * HOP1)
    rows = shape[0] * shape[1] // (CHUNKS * n)
    inputs = inputs.reshape(CHUNKS * n, rows, width)
    cotangent = cotangent.reshape(CHUNKS * n, rows, width)
    flat = (3 * width, width)
    weights = (
        taps_first.reshape(flat), bias_first[None], proj_first, gain_first[None],
        taps_second.reshape(flat), bias_second[None], proj_second, gain_second[None],
    )
    late = (
        taps_first[::-1].transpose(0, 2, 1).reshape(flat), proj_first.T,
        taps_second[::-1].transpose(0, 2, 1).reshape(flat), proj_second.T,
    )

    third = max(1, (n - 1) // 3)
    far, middle, near = (
        range(n - third, n), range(n - 2 * third, n - third), range(1, n - 2 * third)
    )
    order = [s for part in (far, middle, near) for s in reversed(part)]

    picked = [pick(inputs, cotangent, n, chunk) for chunk in range(CHUNKS)]
    first = {s: swap(picked[0][s - 1], "chain", s) for s in order}
    second = {}
    for s in order:
        block = picked[1][s - 1]
        if s in middle:
            partner = s + third
            first[partner], block = lax.optimization_barrier((first[partner], block))
        second[s] = swap(block, "chain", s)
    first = [first[s] for s in range(1, n)]
    second = [second[s] for s in range(1, n)]

    def tie(pieces, part, value):
        held = [pieces[s] for s in part]
        held, value = lax.optimization_barrier((held, value))
        for s, piece in zip(part, held):
            pieces[s] = piece
        return value

    def send_back(pieces):
        return pieces[:1] + [swap(pieces[s], "chain", s) for s in range(1, n)]

    pieces, before = run_chunk(inputs, cotangent, first, weights, late, None, hops, 0)
    pieces, second = lax.optimization_barrier((pieces, second))
    results_a = send_back(pieces)
    pieces, (keep, send) = run_chunk(
        inputs, cotangent, second, weights, late, before[0], hops, 1
    )
    results_b = send_back(pieces)

    send = tie(results_a, far, send)
    got = jnp.concatenate([swap(part, "core") for part in jnp.split(send.reshape(4 * width, width), 1)])
    got = got.reshape(keep.shape)
    half = (keep + got).reshape(2, 2 * width, width)
    parts = jnp.split(take(half, 1 - pair).astype(BF16), 4)
    got = jnp.concatenate([swap(part, "pair") for part in parts])
    quarter = (take(half, pair) + got).reshape(n, 2 * width // n, width)
    quarter = tie(results_a, middle, quarter)
    got = spread(quarter.astype(BF16), place)
    total = take(quarter, place)
    for part in got:
        total = total + part
    total = (total * weight_scale).astype(BF16)
    total = tie(results_b, far, total)
    total = tie(results_a, near, total)
    own = assemble([total] + [swap(total, "chain", s) for s in range(1, n)], place)
    own = own.reshape(2 * width, width)
    by_pair, by_core = swap(own, "pair"), swap(own, "core")
    partial = put(results_a, 0, None)
    partial, by_pair = lax.optimization_barrier((partial, by_pair))
    by_pair = tie(results_b, middle, by_pair)
    by_pair = tie(results_b, near, by_pair)
    by_both = swap(by_pair, "core")
    sums = finish((own, by_pair, by_core, by_both), width)
    outputs, input_grad = put(results_b, 1, partial)
    return (outputs.reshape(shape), input_grad.reshape(shape), *sums)


def solution(mesh):
    groups, seq = mesh.shape["groups"], mesh.shape["seq"]
    own = Mesh(
        mesh.devices.reshape(groups, seq // HOP1, HOP1 // 2, 2),
        ("groups", "chain", "pair", "core"),
    )
    split = P("groups", ("chain", "pair", "core"), None)
    return jax.shard_map(
        on_device,
        mesh=own,
        in_specs=(split, split) + (P(),) * 8,
        out_specs=(
            split,
            split,
            P("groups", None, None),
            P("groups", None, None),
            P("groups", None),
            P("groups", None),
        ),
        check_vma=False,
    )
```

```python
import functools
import math

import jax
import jax.numpy as jnp
from jax import lax
from jax.experimental import pallas as pl
from jax.experimental.pallas import tpu as pltpu
from jax.sharding import Mesh
from jax.sharding import PartitionSpec as P

HOP1 = 4
HOP2 = 8

GELU_COEF = 0.7978845608028654
CUBIC = 0.044715
CHUNKS = 2
VMEM_LIMIT = 60 << 20
BF16 = jnp.bfloat16
F32 = jnp.float32


def gelu_parts(v):
    square = v * v
    th = jnp.tanh(v * (GELU_COEF + (GELU_COEF * CUBIC) * square))
    half = 0.5 + 0.5 * th
    value = v * half
    slope = half + value * (1.0 - th) * (GELU_COEF + (3.0 * CUBIC * GELU_COEF) * square)
    return value, slope


def inverse_rms(x):
    return lax.rsqrt(jnp.mean(x * x, axis=-1, keepdims=True) + 1e-06)


def dot(left, right):
    return jnp.dot(left, right, preferred_element_type=F32)


def row_dot(left, right):
    return lax.dot_general(left, right, (((0,), (0,)), ((), ())), preferred_element_type=F32)


def conv_at(parts, tile, taps, p, n, hop):
    width = parts.shape[-1]
    low = 0 if p - hop >= 0 else 1
    high = 3 if p + hop < n else 2
    left = jnp.concatenate(
        [parts[pl.ds((p + (k - 1) * hop) * tile, tile), :] for k in range(low, high)], axis=-1
    )
    return dot(left, taps[low * width : high * width, :])


def over_rows(total, body, step=64):
    for start in range(0, total, step):
        body(pl.ds(start, step))


def start_all(copies):
    for copy in copies:
        copy.start()
    return copies


def wait_all(copies):
    for copy in copies:
        copy.wait()


def stage(moves, held, sems):
    into, out = [], []
    for i, (source, target) in enumerate(moves):
        into.append(pltpu.make_async_copy(source, held.at[i], sems.at[0, i]))
        out.append(pltpu.make_async_copy(held.at[i], target, sems.at[1, i]))
    start_all(into)
    for arrival, departure in zip(into, out):
        arrival.wait()
        departure.start()
    wait_all(out)


def pick_kernel(n, chunk, inputs, cotangent, *refs):
    pieces, (held, sems) = refs[:-2], refs[-2:]
    me = lax.axis_index("chain")
    moves = [
        (source.at[chunk * n + (me ^ s)], pieces[s - 1].at[k])
        for s in reversed(range(1, n))
        for k, source in enumerate((inputs, cotangent))
    ]
    stage(moves, held, sems)


def pick(inputs, cotangent, n, chunk):
    _, rows, width = inputs.shape
    piece = jax.ShapeDtypeStruct((2, rows, width), BF16)
    return pl.pallas_call(
        functools.partial(pick_kernel, n, chunk),
        name="pick",
        in_specs=in_place(2),
        out_specs=in_place(n - 1),
        out_shape=[piece] * (n - 1),
        scratch_shapes=[
            pltpu.VMEM((2 * (n - 1), rows, width), BF16),
            pltpu.SemaphoreType.DMA((2, 2 * (n - 1))),
        ],
        cost_estimate=small_cost(),
    )(inputs, cotangent)


def put_kernel(n, chunk, fresh, *refs):
    pieces, refs = refs[:n], refs[n if fresh else n + 2 :]
    outs, (held, sems) = refs[:2], refs[2:]
    me = lax.axis_index("chain")
    moves = [
        (pieces[s].at[k], outs[k].at[chunk * n + (me ^ s)]) for s in range(n) for k in range(2)
    ]
    stage(moves, held, sems)


def put(pieces, chunk, into):
    n, (_, rows, width) = len(pieces), pieces[0].shape
    full = jax.ShapeDtypeStruct((CHUNKS * n, rows, width), BF16)
    return pl.pallas_call(
        functools.partial(put_kernel, n, chunk, into is None),
        name="put",
        in_specs=in_place(n if into is None else n + 2),
        out_specs=in_place(2),
        out_shape=[full, full],
        input_output_aliases={} if into is None else {n: 0, n + 1: 1},
        scratch_shapes=[
            pltpu.VMEM((2 * n, rows, width), BF16),
            pltpu.SemaphoreType.DMA((2, 2 * n)),
        ],
        cost_estimate=pl.CostEstimate(
            flops=0, bytes_accessed=16 * n * rows * width, transcendentals=0
        ),
    )(*pieces, *(into or ()))


def finish_kernel(own, by_pair, by_core, by_both, *refs):
    outs, held, sems = refs[:4], refs[4], refs[5]
    pair, core = lax.axis_index("pair"), lax.axis_index("core")
    places = ((core, pair), (core, 1 - pair), (1 - core, pair), (1 - core, 1 - pair))
    wait_all(
        start_all(
            [
                pltpu.make_async_copy(quarter, held.at[block, half], sems.at[i])
                for i, (quarter, (block, half)) in enumerate(
                    zip((own, by_pair, by_core, by_both), places)
                )
            ]
        )
    )
    for block in range(2):
        taps, project = outs[block], outs[2 + block]
        taps[0] = held[block, 0, 0].astype(F32)
        taps[1] = held[block, 0, 1].astype(F32)
        taps[2] = held[block, 1, 0].astype(F32)
        project[...] = held[block, 1, 1].astype(F32)


def finish(quarters, width):
    quarters = [quarter.reshape(2, width, width) for quarter in quarters]
    taps = jax.ShapeDtypeStruct((3, width, width), F32)
    project = jax.ShapeDtypeStruct((width, width), F32)
    return pl.pallas_call(
        finish_kernel,
        name="finish",
        in_specs=in_place(4),
        out_shape=[taps, taps, project, project],
        scratch_shapes=[
            pltpu.VMEM((2, 2, 2, width, width), BF16),
            pltpu.SemaphoreType.DMA((4,)),
        ],
        compiler_params=pltpu.CompilerParams(vmem_limit_bytes=VMEM_LIMIT),
        cost_estimate=small_cost(),
    )(*quarters)


def in_place(count):
    return [pl.BlockSpec(memory_space=pl.ANY)] * count


def small_cost():
    return pl.CostEstimate(flops=1000, bytes_accessed=1000, transcendentals=0)


def chunk_kernel(n, hops, chunk, last, *refs):
    inputs, cotangent, refs = refs[0], refs[1], refs[2:]
    pieces, weights, late, refs = refs[: n - 1], refs[n - 1 : n + 7], refs[n + 7 : n + 11], refs[n + 11 :]
    if last:
        before, refs = refs[0], refs[1:]
    piece_outs, refs = refs[:n], refs[n:]
    if last:
        keep_out, send_out, sums = refs[:3]
        refs = refs[3:]
    else:
        sums, refs = refs[0], refs[1:]
    sources, grad, wide, hidden_grad, acts, gelleds, norm_slopes, hidden_slopes = refs[:8]
    late_held, sems, late_sems = refs[8:12], refs[12], refs[13]
    me, core = lax.axis_index("chain"), lax.axis_index("core")
    _, rows_in, width = inputs.shape
    tile, total = rows_in, n * rows_in

    def place(s):
        return pl.ds(pl.multiple_of((me ^ s) * tile, tile), tile)

    def arriving(k, held, whole_array):
        copies = []
        for s in range(n):
            source = whole_array.at[chunk * n + me] if s == 0 else pieces[s - 1].at[k]
            copies.append(pltpu.make_async_copy(source, held.at[place(s), :], sems.at[k, s]))
        return start_all(copies)

    def leaving(k, held):
        copies = []
        for s in range(n):
            copies.append(
                pltpu.make_async_copy(
                    held.at[place(s), :], piece_outs[s].at[k], sems.at[2 + k, s]
                )
            )
        return start_all(copies)

    x_copies = arriving(0, sources.at[0], inputs)
    late_copies = start_all(
        [
            pltpu.make_async_copy(source, held, late_sems.at[i])
            for i, (source, held) in enumerate(zip(late, late_held))
        ]
    )
    y_copies = arriving(1, grad, cotangent)
    if last:
        late_copies += start_all([pltpu.make_async_copy(before, sums, late_sems.at[4])])
    wait_all(x_copies)

    for block in range(2):
        taps, bias, project, gain = weights[4 * block : 4 * block + 4]
        gain_row, bias_row = gain[...], bias[...]

        def before_conv(rows):
            x = sources[block, rows, :].astype(F32)
            value, slope = gelu_parts(x * inverse_rms(x) * gain_row)
            acts[block, rows, :] = value.astype(BF16)
            norm_slopes[block, rows, :] = slope * gain_row

        over_rows(total, before_conv)
        for p in range(n):
            wide[pl.ds(p * tile, tile), :] = conv_at(
                acts.at[block], tile, taps, p, n, hops[block]
            )

        def after_conv(rows):
            value, slope = gelu_parts(wide[rows, :] + bias_row)
            gelleds[block, rows, :] = value.astype(BF16)
            hidden_slopes[block, rows, :] = slope

        over_rows(total, after_conv)
        sources[block + 1] = (
            sources[block].astype(F32) + dot(gelleds[block], project[...])
        ).astype(BF16)

    out_copies = leaving(0, sources.at[2])
    wait_all(y_copies + late_copies)

    def add(k, value):
        sums[k] = sums[k] + value if last else value

    for block in (1, 0):
        taps_t, project_t = late_held[2 * block : 2 * block + 2]
        hop = hops[block]
        cut = hop * tile
        add(4 * block + 3, row_dot(gelleds[block], grad[...]))
        wide[...] = dot(grad[...], project_t[...])

        def hidden_rows(rows):
            hidden_grad[rows, :] = (wide[rows, :] * hidden_slopes[block, rows, :]).astype(BF16)

        over_rows(total, hidden_rows)
        add(4 * block, row_dot(acts[block, : total - cut, :], hidden_grad[cut:, :]))
        add(4 * block + 1, row_dot(acts[block], hidden_grad[...]))
        add(4 * block + 2, row_dot(acts[block, cut:, :], hidden_grad[: total - cut, :]))
        for p in range(n):
            wide[pl.ds(p * tile, tile), :] = conv_at(hidden_grad, tile, taps_t, p, n, hop)

        def source_rows(rows):
            weighted = wide[rows, :] * norm_slopes[block, rows, :]
            x = sources[block, rows, :].astype(F32)
            inv = inverse_rms(x)
            unit = x * inv
            mean = jnp.mean(unit * weighted, axis=-1, keepdims=True)
            grad[rows, :] = (
                grad[rows, :].astype(F32) + inv * (weighted - unit * mean)
            ).astype(BF16)

        over_rows(total, source_rows)

    out_copies += leaving(1, grad)
    if last:
        keep_out[...] = sums[pl.ds(4 * core, 4)]
        send_out[...] = sums[pl.ds(4 * (1 - core), 4)].astype(BF16)
    wait_all(out_copies)


def run_chunk(inputs, cotangent, pieces, weights, late, before, hops, chunk):
    n, (_, rows, width) = len(pieces) + 1, pieces[0].shape
    last = before is not None
    total = n * rows
    full = jax.ShapeDtypeStruct((8, width, width), F32)
    half = (4, width, width)
    sums = [jax.ShapeDtypeStruct(half, F32), jax.ShapeDtypeStruct(half, BF16)] if last else [full]
    operands = [inputs, cotangent, *pieces, *weights, *late] + ([before] if last else [])
    scratch = [pltpu.VMEM(full.shape, F32)] if last else []
    outs = pl.pallas_call(
        functools.partial(chunk_kernel, n, hops, chunk, last),
        name="chunk",
        in_specs=in_place(n + 1)
        + [pl.BlockSpec(weight.shape, None) for weight in weights]
        + in_place(5 if last else 4),
        out_specs=in_place(n) + [pl.BlockSpec(kind.shape, None) for kind in sums],
        out_shape=[jax.ShapeDtypeStruct(pieces[0].shape, BF16)] * n + sums,
        scratch_shapes=scratch
        + [
            pltpu.VMEM((3, total, width), BF16),
            pltpu.VMEM((total, width), BF16),
            pltpu.VMEM((total, width), F32),
            pltpu.VMEM((total, width), BF16),
            pltpu.VMEM((2, total, width), BF16),
            pltpu.VMEM((2, total, width), BF16),
            pltpu.VMEM((2, total, width), F32),
            pltpu.VMEM((2, total, width), F32),
        ]
        + [pltpu.VMEM(weight.shape, BF16) for weight in late]
        + [pltpu.SemaphoreType.DMA((4, n)), pltpu.SemaphoreType.DMA((5,))],
        compiler_params=pltpu.CompilerParams(vmem_limit_bytes=VMEM_LIMIT),
        cost_estimate=small_cost(),
    )(*operands)
    return list(outs[:n]), list(outs[n:])


def take(array, index):
    return lax.dynamic_index_in_dim(array, index, 0, keepdims=False)


def swap(values, axis, s=1):
    return lax.ppermute(values, axis, [(i, i ^ s) for i in range(lax.axis_size(axis))])


def spread(array, me):
    n = array.shape[0]
    return [swap(take(array, me ^ s), "chain", s) for s in range(1, n)]


def assemble(pieces, me):
    out = jnp.stack(pieces)
    return jnp.take(out, me ^ jnp.arange(len(pieces)), axis=0)


def on_device(
    inputs,
    cotangent,
    taps_first,
    taps_second,
    bias_first,
    bias_second,
    proj_first,
    proj_second,
    gain_first,
    gain_second,
):
    n = lax.axis_size("chain")
    place, pair = lax.axis_index("chain"), lax.axis_index("pair")
    hops = (1, HOP2 // HOP1)
    shape = inputs.shape
    width = shape[-1]
    weight_scale = 1.0 / math.sqrt(shape[0] * shape[1] * n * HOP1)
    rows = shape[0] * shape[1] // (CHUNKS * n)
    inputs = inputs.reshape(CHUNKS * n, rows, width)
    cotangent = cotangent.reshape(CHUNKS * n, rows, width)
    flat = (3 * width, width)
    weights = (
        taps_first.reshape(flat), bias_first[None], proj_first, gain_first[None],
        taps_second.reshape(flat), bias_second[None], proj_second, gain_second[None],
    )
    late = (
        taps_first[::-1].transpose(0, 2, 1).reshape(flat), proj_first.T,
        taps_second[::-1].transpose(0, 2, 1).reshape(flat), proj_second.T,
    )

    third = max(1, (n - 1) // 3)
    far, middle, near = (
        range(n - third, n), range(n - 2 * third, n - third), range(1, n - 2 * third)
    )
    order = [s for part in (far, middle, near) for s in reversed(part)]

    picked = [pick(inputs, cotangent, n, chunk) for chunk in range(CHUNKS)]
    first = {s: swap(picked[0][s - 1], "chain", s) for s in order}
    second = {}
    for s in order:
        block = picked[1][s - 1]
        if s in middle:
            partner = s + third
            first[partner], block = lax.optimization_barrier((first[partner], block))
        second[s] = swap(block, "chain", s)
    first = [first[s] for s in range(1, n)]
    second = [second[s] for s in range(1, n)]

    def tie(pieces, part, value):
        held = [pieces[s] for s in part]
        held, value = lax.optimization_barrier((held, value))
        for s, piece in zip(part, held):
            pieces[s] = piece
        return value

    def send_back(pieces):
        return pieces[:1] + [swap(pieces[s], "chain", s) for s in range(1, n)]

    pieces, before = run_chunk(inputs, cotangent, first, weights, late, None, hops, 0)
    pieces, second = lax.optimization_barrier((pieces, second))
    results_a = send_back(pieces)
    pieces, (keep, send) = run_chunk(
        inputs, cotangent, second, weights, late, before[0], hops, 1
    )
    results_b = send_back(pieces)

    send = tie(results_a, far, send)
    got = jnp.concatenate([swap(part, "core") for part in jnp.split(send.reshape(4 * width, width), 1)])
    got = got.reshape(keep.shape)
    half = (keep + got).reshape(2, 2 * width, width)
    parts = jnp.split(take(half, 1 - pair).astype(BF16), 4)
    got = jnp.concatenate([swap(part, "pair") for part in parts])
    quarter = (take(half, pair) + got).reshape(n, 2 * width // n, width)
    quarter = tie(results_a, middle, quarter)
    got = spread(quarter.astype(BF16), place)
    total = take(quarter, place)
    for part in got:
        total = total + part
    total = (total * weight_scale).astype(BF16)
    total = tie(results_b, far, total)
    total = tie(results_a, near, total)
    own = assemble([total] + [swap(total, "chain", s) for s in range(1, n)], place)
    own = own.reshape(2 * width, width)
    by_pair, by_core = swap(own, "pair"), swap(own, "core")
    partial = put(results_a, 0, None)
    by_both = lax.ppermute(own, ("pair", "core"), [(i, i ^ 3) for i in range(4)])
    sums = finish((own, by_pair, by_core, by_both), width)
    sums, partial = lax.optimization_barrier((sums, partial))
    outputs, input_grad = put(results_b, 1, partial)
    return (outputs.reshape(shape), input_grad.reshape(shape), *sums)


def solution(mesh):
    groups, seq = mesh.shape["groups"], mesh.shape["seq"]
    own = Mesh(
        mesh.devices.reshape(groups, seq // HOP1, HOP1 // 2, 2),
        ("groups", "chain", "pair", "core"),
    )
    split = P("groups", ("chain", "pair", "core"), None)
    return jax.shard_map(
        on_device,
        mesh=own,
        in_specs=(split, split) + (P(),) * 8,
        out_specs=(
            split,
            split,
            P("groups", None, None),
            P("groups", None, None),
            P("groups", None),
            P("groups", None),
        ),
        check_vma=False,
    )
```

```python
import functools
import math

import jax
import jax.numpy as jnp
from jax import lax
from jax.experimental import pallas as pl
from jax.experimental.pallas import tpu as pltpu
from jax.sharding import Mesh
from jax.sharding import PartitionSpec as P

HOP1 = 4
HOP2 = 8

GELU_COEF = 0.7978845608028654
CUBIC = 0.044715
CHUNKS = 2
VMEM_LIMIT = 60 << 20
BF16 = jnp.bfloat16
F32 = jnp.float32


def gelu_parts(v):
    square = v * v
    th = jnp.tanh(v * (GELU_COEF + (GELU_COEF * CUBIC) * square))
    half = 0.5 + 0.5 * th
    value = v * half
    slope = half + value * (1.0 - th) * (GELU_COEF + (3.0 * CUBIC * GELU_COEF) * square)
    return value, slope


def inverse_rms(x):
    return lax.rsqrt(jnp.mean(x * x, axis=-1, keepdims=True) + 1e-06)


def dot(left, right):
    return jnp.dot(left, right, preferred_element_type=F32)


def row_dot(left, right):
    return lax.dot_general(left, right, (((0,), (0,)), ((), ())), preferred_element_type=F32)


def conv_at(parts, tile, taps, p, n, hop):
    width = parts.shape[-1]
    low = 0 if p - hop >= 0 else 1
    high = 3 if p + hop < n else 2
    left = jnp.concatenate(
        [parts[pl.ds((p + (k - 1) * hop) * tile, tile), :] for k in range(low, high)], axis=-1
    )
    return dot(left, taps[low * width : high * width, :])


def over_rows(total, body, step=64):
    for start in range(0, total, step):
        body(pl.ds(start, step))


def start_all(copies):
    for copy in copies:
        copy.start()
    return copies


def wait_all(copies):
    for copy in copies:
        copy.wait()


def stage(moves, held, sems):
    into, out = [], []
    for i, (source, target) in enumerate(moves):
        into.append(pltpu.make_async_copy(source, held.at[i], sems.at[0, i]))
        out.append(pltpu.make_async_copy(held.at[i], target, sems.at[1, i]))
    start_all(into)
    for arrival, departure in zip(into, out):
        arrival.wait()
        departure.start()
    wait_all(out)


def pick_kernel(n, chunk, inputs, cotangent, *refs):
    pieces, (held, sems) = refs[:-2], refs[-2:]
    me = lax.axis_index("chain")
    moves = [
        (source.at[chunk * n + (me ^ s)], pieces[s - 1].at[k])
        for s in reversed(range(1, n))
        for k, source in enumerate((inputs, cotangent))
    ]
    stage(moves, held, sems)


def pick(inputs, cotangent, n, chunk):
    _, rows, width = inputs.shape
    piece = jax.ShapeDtypeStruct((2, rows, width), BF16)
    return pl.pallas_call(
        functools.partial(pick_kernel, n, chunk),
        name="pick",
        in_specs=in_place(2),
        out_specs=in_place(n - 1),
        out_shape=[piece] * (n - 1),
        scratch_shapes=[
            pltpu.VMEM((2 * (n - 1), rows, width), BF16),
            pltpu.SemaphoreType.DMA((2, 2 * (n - 1))),
        ],
        cost_estimate=small_cost(),
    )(inputs, cotangent)


def put_kernel(n, chunk, fresh, *refs):
    pieces, refs = refs[:n], refs[n if fresh else n + 2 :]
    outs, (held, sems) = refs[:2], refs[2:]
    me = lax.axis_index("chain")
    moves = [
        (pieces[s].at[k], outs[k].at[chunk * n + (me ^ s)]) for s in range(n) for k in range(2)
    ]
    stage(moves, held, sems)


def put(pieces, chunk, into):
    n, (_, rows, width) = len(pieces), pieces[0].shape
    full = jax.ShapeDtypeStruct((CHUNKS * n, rows, width), BF16)
    return pl.pallas_call(
        functools.partial(put_kernel, n, chunk, into is None),
        name="put",
        in_specs=in_place(n if into is None else n + 2),
        out_specs=in_place(2),
        out_shape=[full, full],
        input_output_aliases={} if into is None else {n: 0, n + 1: 1},
        scratch_shapes=[
            pltpu.VMEM((2 * n, rows, width), BF16),
            pltpu.SemaphoreType.DMA((2, 2 * n)),
        ],
        compiler_params=pltpu.CompilerParams(vmem_limit_bytes=8 << 20),
        cost_estimate=pl.CostEstimate(
            flops=0, bytes_accessed=16 * n * rows * width, transcendentals=0
        ),
    )(*pieces, *(into or ()))


def finish_kernel(own, by_pair, by_core, by_both, *refs):
    outs, held, sems = refs[:4], refs[4], refs[5]
    pair, core = lax.axis_index("pair"), lax.axis_index("core")
    places = ((core, pair), (core, 1 - pair), (1 - core, pair), (1 - core, 1 - pair))
    wait_all(
        start_all(
            [
                pltpu.make_async_copy(quarter, held.at[block, half], sems.at[i])
                for i, (quarter, (block, half)) in enumerate(
                    zip((own, by_pair, by_core, by_both), places)
                )
            ]
        )
    )
    for block in range(2):
        taps, project = outs[block], outs[2 + block]
        taps[0] = held[block, 0, 0].astype(F32)
        taps[1] = held[block, 0, 1].astype(F32)
        taps[2] = held[block, 1, 0].astype(F32)
        project[...] = held[block, 1, 1].astype(F32)


def finish(quarters, width):
    quarters = [quarter.reshape(2, width, width) for quarter in quarters]
    taps = jax.ShapeDtypeStruct((3, width, width), F32)
    project = jax.ShapeDtypeStruct((width, width), F32)
    return pl.pallas_call(
        finish_kernel,
        name="finish",
        in_specs=in_place(4),
        out_shape=[taps, taps, project, project],
        scratch_shapes=[
            pltpu.VMEM((2, 2, 2, width, width), BF16),
            pltpu.SemaphoreType.DMA((4,)),
        ],
        compiler_params=pltpu.CompilerParams(vmem_limit_bytes=8 << 20),
        cost_estimate=small_cost(),
    )(*quarters)


def in_place(count):
    return [pl.BlockSpec(memory_space=pl.ANY)] * count


def small_cost():
    return pl.CostEstimate(flops=1000, bytes_accessed=1000, transcendentals=0)


def chunk_kernel(n, hops, chunk, last, *refs):
    inputs, cotangent, refs = refs[0], refs[1], refs[2:]
    pieces, weights, late, refs = refs[: n - 1], refs[n - 1 : n + 7], refs[n + 7 : n + 11], refs[n + 11 :]
    if last:
        before, refs = refs[0], refs[1:]
    piece_outs, refs = refs[:n], refs[n:]
    if last:
        keep_out, send_out, sums = refs[:3]
        refs = refs[3:]
    else:
        sums, refs = refs[0], refs[1:]
    sources, grad, wide, hidden_grad, acts, gelleds, norm_slopes, hidden_slopes = refs[:8]
    late_held, sems, late_sems = refs[8:12], refs[12], refs[13]
    me, core = lax.axis_index("chain"), lax.axis_index("core")
    _, rows_in, width = inputs.shape
    tile, total = rows_in, n * rows_in

    def place(s):
        return pl.ds(pl.multiple_of((me ^ s) * tile, tile), tile)

    def arriving(k, held, whole_array):
        copies = []
        for s in range(n):
            source = whole_array.at[chunk * n + me] if s == 0 else pieces[s - 1].at[k]
            copies.append(pltpu.make_async_copy(source, held.at[place(s), :], sems.at[k, s]))
        return start_all(copies)

    def leaving(k, held):
        copies = []
        for s in range(n):
            copies.append(
                pltpu.make_async_copy(
                    held.at[place(s), :], piece_outs[s].at[k], sems.at[2 + k, s]
                )
            )
        return start_all(copies)

    x_copies = arriving(0, sources.at[0], inputs)
    late_copies = start_all(
        [
            pltpu.make_async_copy(source, held, late_sems.at[i])
            for i, (source, held) in enumerate(zip(late, late_held))
        ]
    )
    y_copies = arriving(1, grad, cotangent)
    if last:
        late_copies += start_all([pltpu.make_async_copy(before, sums, late_sems.at[4])])
    wait_all(x_copies)

    for block in range(2):
        taps, bias, project, gain = weights[4 * block : 4 * block + 4]
        gain_row, bias_row = gain[...], bias[...]

        def before_conv(rows):
            x = sources[block, rows, :].astype(F32)
            value, slope = gelu_parts(x * inverse_rms(x) * gain_row)
            acts[block, rows, :] = value.astype(BF16)
            norm_slopes[block, rows, :] = slope * gain_row

        over_rows(total, before_conv)
        for p in range(n):
            wide[pl.ds(p * tile, tile), :] = conv_at(
                acts.at[block], tile, taps, p, n, hops[block]
            )

        def after_conv(rows):
            value, slope = gelu_parts(wide[rows, :] + bias_row)
            gelleds[block, rows, :] = value.astype(BF16)
            hidden_slopes[block, rows, :] = slope

        over_rows(total, after_conv)
        sources[block + 1] = (
            sources[block].astype(F32) + dot(gelleds[block], project[...])
        ).astype(BF16)

    out_copies = leaving(0, sources.at[2])
    wait_all(y_copies + late_copies)

    def add(k, value):
        sums[k] = sums[k] + value if last else value

    for block in (1, 0):
        taps_t, project_t = late_held[2 * block : 2 * block + 2]
        hop = hops[block]
        cut = hop * tile
        add(4 * block + 3, row_dot(gelleds[block], grad[...]))
        wide[...] = dot(grad[...], project_t[...])

        def hidden_rows(rows):
            hidden_grad[rows, :] = (wide[rows, :] * hidden_slopes[block, rows, :]).astype(BF16)

        over_rows(total, hidden_rows)
        add(4 * block, row_dot(acts[block, : total - cut, :], hidden_grad[cut:, :]))
        add(4 * block + 1, row_dot(acts[block], hidden_grad[...]))
        add(4 * block + 2, row_dot(acts[block, cut:, :], hidden_grad[: total - cut, :]))
        for p in range(n):
            wide[pl.ds(p * tile, tile), :] = conv_at(hidden_grad, tile, taps_t, p, n, hop)

        def source_rows(rows):
            weighted = wide[rows, :] * norm_slopes[block, rows, :]
            x = sources[block, rows, :].astype(F32)
            inv = inverse_rms(x)
            unit = x * inv
            mean = jnp.mean(unit * weighted, axis=-1, keepdims=True)
            grad[rows, :] = (
                grad[rows, :].astype(F32) + inv * (weighted - unit * mean)
            ).astype(BF16)

        over_rows(total, source_rows)

    out_copies += leaving(1, grad)
    if last:
        keep_out[...] = sums[pl.ds(4 * core, 4)]
        send_out[...] = sums[pl.ds(4 * (1 - core), 4)].astype(BF16)
    wait_all(out_copies)


def run_chunk(inputs, cotangent, pieces, weights, late, before, hops, chunk):
    n, (_, rows, width) = len(pieces) + 1, pieces[0].shape
    last = before is not None
    total = n * rows
    full = jax.ShapeDtypeStruct((8, width, width), F32)
    half = (4, width, width)
    sums = [jax.ShapeDtypeStruct(half, F32), jax.ShapeDtypeStruct(half, BF16)] if last else [full]
    operands = [inputs, cotangent, *pieces, *weights, *late] + ([before] if last else [])
    scratch = [pltpu.VMEM(full.shape, F32)] if last else []
    outs = pl.pallas_call(
        functools.partial(chunk_kernel, n, hops, chunk, last),
        name="chunk",
        in_specs=in_place(n + 1)
        + [pl.BlockSpec(weight.shape, None) for weight in weights]
        + in_place(5 if last else 4),
        out_specs=in_place(n) + [pl.BlockSpec(kind.shape, None) for kind in sums],
        out_shape=[jax.ShapeDtypeStruct(pieces[0].shape, BF16)] * n + sums,
        scratch_shapes=scratch
        + [
            pltpu.VMEM((3, total, width), BF16),
            pltpu.VMEM((total, width), BF16),
            pltpu.VMEM((total, width), F32),
            pltpu.VMEM((total, width), BF16),
            pltpu.VMEM((2, total, width), BF16),
            pltpu.VMEM((2, total, width), BF16),
            pltpu.VMEM((2, total, width), F32),
            pltpu.VMEM((2, total, width), F32),
        ]
        + [pltpu.VMEM(weight.shape, BF16) for weight in late]
        + [pltpu.SemaphoreType.DMA((4, n)), pltpu.SemaphoreType.DMA((5,))],
        compiler_params=pltpu.CompilerParams(vmem_limit_bytes=VMEM_LIMIT),
        cost_estimate=small_cost(),
    )(*operands)
    return list(outs[:n]), list(outs[n:])


def take(array, index):
    return lax.dynamic_index_in_dim(array, index, 0, keepdims=False)


def swap(values, axis, s=1):
    return lax.ppermute(values, axis, [(i, i ^ s) for i in range(lax.axis_size(axis))])


def spread(array, me):
    n = array.shape[0]
    return [swap(take(array, me ^ s), "chain", s) for s in range(1, n)]


def assemble(pieces, me):
    out = jnp.stack(pieces)
    return jnp.take(out, me ^ jnp.arange(len(pieces)), axis=0)


def on_device(
    inputs,
    cotangent,
    taps_first,
    taps_second,
    bias_first,
    bias_second,
    proj_first,
    proj_second,
    gain_first,
    gain_second,
):
    n = lax.axis_size("chain")
    place, pair = lax.axis_index("chain"), lax.axis_index("pair")
    hops = (1, HOP2 // HOP1)
    shape = inputs.shape
    width = shape[-1]
    weight_scale = 1.0 / math.sqrt(shape[0] * shape[1] * n * HOP1)
    rows = shape[0] * shape[1] // (CHUNKS * n)
    inputs = inputs.reshape(CHUNKS * n, rows, width)
    cotangent = cotangent.reshape(CHUNKS * n, rows, width)
    flat = (3 * width, width)
    weights = (
        taps_first.reshape(flat), bias_first[None], proj_first, gain_first[None],
        taps_second.reshape(flat), bias_second[None], proj_second, gain_second[None],
    )
    late = (
        taps_first[::-1].transpose(0, 2, 1).reshape(flat), proj_first.T,
        taps_second[::-1].transpose(0, 2, 1).reshape(flat), proj_second.T,
    )

    third = max(1, (n - 1) // 3)
    far, middle, near = (
        range(n - third, n), range(n - 2 * third, n - third), range(1, n - 2 * third)
    )
    order = [s for part in (far, middle, near) for s in reversed(part)]

    picked = [pick(inputs, cotangent, n, chunk) for chunk in range(CHUNKS)]
    first = {s: swap(picked[0][s - 1], "chain", s) for s in order}
    second = {}
    for s in order:
        block = picked[1][s - 1]
        if s in middle:
            partner = s + third
            first[partner], block = lax.optimization_barrier((first[partner], block))
        second[s] = swap(block, "chain", s)
    first = [first[s] for s in range(1, n)]
    second = [second[s] for s in range(1, n)]

    def tie(pieces, part, value):
        held = [pieces[s] for s in part]
        held, value = lax.optimization_barrier((held, value))
        for s, piece in zip(part, held):
            pieces[s] = piece
        return value

    def send_back(pieces):
        return pieces[:1] + [swap(pieces[s], "chain", s) for s in range(1, n)]

    pieces, before = run_chunk(inputs, cotangent, first, weights, late, None, hops, 0)
    pieces, second = lax.optimization_barrier((pieces, second))
    results_a = send_back(pieces)
    pieces, (keep, send) = run_chunk(
        inputs, cotangent, second, weights, late, before[0], hops, 1
    )
    results_b = send_back(pieces)

    send = tie(results_a, far, send)
    got = jnp.concatenate([swap(part, "core") for part in jnp.split(send.reshape(4 * width, width), 1)])
    got = got.reshape(keep.shape)
    half = (keep + got).reshape(2, 2 * width, width)
    parts = jnp.split(take(half, 1 - pair).astype(BF16), 4)
    got = jnp.concatenate([swap(part, "pair") for part in parts])
    quarter = (take(half, pair) + got).reshape(n, 2 * width // n, width)
    quarter = tie(results_a, middle, quarter)
    got = spread(quarter.astype(BF16), place)
    total = take(quarter, place)
    for part in got:
        total = total + part
    total = (total * weight_scale).astype(BF16)
    total = tie(results_b, far, total)
    total = tie(results_a, near, total)
    own = assemble([total] + [swap(total, "chain", s) for s in range(1, n)], place)
    own = own.reshape(2 * width, width)
    by_pair, by_core = swap(own, "pair"), swap(own, "core")
    partial = put(results_a, 0, None)
    by_both = lax.ppermute(own, ("pair", "core"), [(i, i ^ 3) for i in range(4)])
    sums = finish((own, by_pair, by_core, by_both), width)
    sums, partial = lax.optimization_barrier((sums, partial))
    outputs, input_grad = put(results_b, 1, partial)
    return (outputs.reshape(shape), input_grad.reshape(shape), *sums)


def solution(mesh):
    groups, seq = mesh.shape["groups"], mesh.shape["seq"]
    own = Mesh(
        mesh.devices.reshape(groups, seq // HOP1, HOP1 // 2, 2),
        ("groups", "chain", "pair", "core"),
    )
    split = P("groups", ("chain", "pair", "core"), None)
    return jax.shard_map(
        on_device,
        mesh=own,
        in_specs=(split, split) + (P(),) * 8,
        out_specs=(
            split,
            split,
            P("groups", None, None),
            P("groups", None, None),
            P("groups", None),
            P("groups", None),
        ),
        check_vma=False,
    )
```

```python
import functools
import math

import jax
import jax.numpy as jnp
from jax import lax
from jax.experimental import pallas as pl
from jax.experimental.pallas import tpu as pltpu
from jax.sharding import Mesh
from jax.sharding import PartitionSpec as P

HOP1 = 4
HOP2 = 8

GELU_COEF = 0.7978845608028654
CUBIC = 0.044715
CHUNKS = 2
VMEM_LIMIT = 60 << 20
BF16 = jnp.bfloat16
F32 = jnp.float32


def gelu_parts(v):
    square = v * v
    th = jnp.tanh(v * (GELU_COEF + (GELU_COEF * CUBIC) * square))
    half = 0.5 + 0.5 * th
    value = v * half
    slope = half + value * (1.0 - th) * (GELU_COEF + (3.0 * CUBIC * GELU_COEF) * square)
    return value, slope


def inverse_rms(x):
    return lax.rsqrt(jnp.mean(x * x, axis=-1, keepdims=True) + 1e-06)


def dot(left, right):
    return jnp.dot(left, right, preferred_element_type=F32)


def row_dot(left, right):
    return lax.dot_general(left, right, (((0,), (0,)), ((), ())), preferred_element_type=F32)


def conv_at(parts, tile, taps, p, n, hop):
    width = parts.shape[-1]
    low = 0 if p - hop >= 0 else 1
    high = 3 if p + hop < n else 2
    left = jnp.concatenate(
        [parts[pl.ds((p + (k - 1) * hop) * tile, tile), :] for k in range(low, high)], axis=-1
    )
    return dot(left, taps[low * width : high * width, :])


def over_rows(total, body, step=64):
    for start in range(0, total, step):
        body(pl.ds(start, step))


def start_all(copies):
    for copy in copies:
        copy.start()
    return copies


def wait_all(copies):
    for copy in copies:
        copy.wait()


def stage(moves, held, sems):
    into, out = [], []
    for i, (source, target) in enumerate(moves):
        into.append(pltpu.make_async_copy(source, held.at[i], sems.at[0, i]))
        out.append(pltpu.make_async_copy(held.at[i], target, sems.at[1, i]))
    start_all(into)
    for arrival, departure in zip(into, out):
        arrival.wait()
        departure.start()
    wait_all(out)


def pick_kernel(n, chunk, order, inputs, cotangent, *refs):
    pieces, (held, sems) = refs[:-2], refs[-2:]
    me = lax.axis_index("chain")
    moves = [
        (source.at[chunk * n + (me ^ s)], pieces[i].at[k])
        for i, s in enumerate(order)
        for k, source in enumerate((inputs, cotangent))
    ]
    stage(moves, held, sems)


def pick(inputs, cotangent, n, chunk, order):
    _, rows, width = inputs.shape
    piece = jax.ShapeDtypeStruct((2, rows, width), BF16)
    return pl.pallas_call(
        functools.partial(pick_kernel, n, chunk, order),
        name="pick",
        in_specs=in_place(2),
        out_specs=in_place(len(order)),
        out_shape=[piece] * len(order),
        scratch_shapes=[
            pltpu.VMEM((2 * len(order), rows, width), BF16),
            pltpu.SemaphoreType.DMA((2, 2 * len(order))),
        ],
        cost_estimate=small_cost(),
    )(inputs, cotangent)


def put_kernel(n, chunk, fresh, *refs):
    pieces, refs = refs[:n], refs[n if fresh else n + 2 :]
    outs, (held, sems) = refs[:2], refs[2:]
    me = lax.axis_index("chain")
    moves = [
        (pieces[s].at[k], outs[k].at[chunk * n + (me ^ s)]) for s in range(n) for k in range(2)
    ]
    stage(moves, held, sems)


def put(pieces, chunk, into):
    n, (_, rows, width) = len(pieces), pieces[0].shape
    full = jax.ShapeDtypeStruct((CHUNKS * n, rows, width), BF16)
    return pl.pallas_call(
        functools.partial(put_kernel, n, chunk, into is None),
        name="put",
        in_specs=in_place(n if into is None else n + 2),
        out_specs=in_place(2),
        out_shape=[full, full],
        input_output_aliases={} if into is None else {n: 0, n + 1: 1},
        scratch_shapes=[
            pltpu.VMEM((2 * n, rows, width), BF16),
            pltpu.SemaphoreType.DMA((2, 2 * n)),
        ],
        compiler_params=pltpu.CompilerParams(vmem_limit_bytes=8 << 20),
        cost_estimate=pl.CostEstimate(
            flops=0, bytes_accessed=16 * n * rows * width, transcendentals=0
        ),
    )(*pieces, *(into or ()))


def finish_kernel(own, by_pair, by_core, by_both, *refs):
    outs, held, sems = refs[:4], refs[4], refs[5]
    pair, core = lax.axis_index("pair"), lax.axis_index("core")
    places = ((core, pair), (core, 1 - pair), (1 - core, pair), (1 - core, 1 - pair))
    wait_all(
        start_all(
            [
                pltpu.make_async_copy(quarter, held.at[block, half], sems.at[i])
                for i, (quarter, (block, half)) in enumerate(
                    zip((own, by_pair, by_core, by_both), places)
                )
            ]
        )
    )
    for block in range(2):
        taps, project = outs[block], outs[2 + block]
        taps[0] = held[block, 0, 0].astype(F32)
        taps[1] = held[block, 0, 1].astype(F32)
        taps[2] = held[block, 1, 0].astype(F32)
        project[...] = held[block, 1, 1].astype(F32)


def finish(quarters, width):
    quarters = [quarter.reshape(2, width, width) for quarter in quarters]
    taps = jax.ShapeDtypeStruct((3, width, width), F32)
    project = jax.ShapeDtypeStruct((width, width), F32)
    return pl.pallas_call(
        finish_kernel,
        name="finish",
        in_specs=in_place(4),
        out_shape=[taps, taps, project, project],
        scratch_shapes=[
            pltpu.VMEM((2, 2, 2, width, width), BF16),
            pltpu.SemaphoreType.DMA((4,)),
        ],
        compiler_params=pltpu.CompilerParams(vmem_limit_bytes=8 << 20),
        cost_estimate=small_cost(),
    )(*quarters)


def in_place(count):
    return [pl.BlockSpec(memory_space=pl.ANY)] * count


def small_cost():
    return pl.CostEstimate(flops=1000, bytes_accessed=1000, transcendentals=0)


def chunk_kernel(n, hops, chunk, last, *refs):
    inputs, cotangent, refs = refs[0], refs[1], refs[2:]
    pieces, weights, late, refs = refs[: n - 1], refs[n - 1 : n + 7], refs[n + 7 : n + 11], refs[n + 11 :]
    if last:
        before, refs = refs[0], refs[1:]
    piece_outs, refs = refs[:n], refs[n:]
    if last:
        keep_out, send_out, sums = refs[:3]
        refs = refs[3:]
    else:
        sums, refs = refs[0], refs[1:]
    sources, grad, wide, hidden_grad, acts, gelleds, norm_slopes, hidden_slopes = refs[:8]
    late_held, sems, late_sems = refs[8:12], refs[12], refs[13]
    me, core = lax.axis_index("chain"), lax.axis_index("core")
    _, rows_in, width = inputs.shape
    tile, total = rows_in, n * rows_in

    def place(s):
        return pl.ds(pl.multiple_of((me ^ s) * tile, tile), tile)

    def arriving(k, held, whole_array):
        copies = []
        for s in range(n):
            source = whole_array.at[chunk * n + me] if s == 0 else pieces[s - 1].at[k]
            copies.append(pltpu.make_async_copy(source, held.at[place(s), :], sems.at[k, s]))
        return start_all(copies)

    def leaving(k, held):
        copies = []
        for s in range(n):
            copies.append(
                pltpu.make_async_copy(
                    held.at[place(s), :], piece_outs[s].at[k], sems.at[2 + k, s]
                )
            )
        return start_all(copies)

    x_copies = arriving(0, sources.at[0], inputs)
    late_copies = start_all(
        [
            pltpu.make_async_copy(source, held, late_sems.at[i])
            for i, (source, held) in enumerate(zip(late, late_held))
        ]
    )
    y_copies = arriving(1, grad, cotangent)
    if last:
        late_copies += start_all([pltpu.make_async_copy(before, sums, late_sems.at[4])])
    wait_all(x_copies)

    for block in range(2):
        taps, bias, project, gain = weights[4 * block : 4 * block + 4]
        gain_row, bias_row = gain[...], bias[...]

        def before_conv(rows):
            x = sources[block, rows, :].astype(F32)
            value, slope = gelu_parts(x * inverse_rms(x) * gain_row)
            acts[block, rows, :] = value.astype(BF16)
            norm_slopes[block, rows, :] = slope * gain_row

        over_rows(total, before_conv)
        for p in range(n):
            wide[pl.ds(p * tile, tile), :] = conv_at(
                acts.at[block], tile, taps, p, n, hops[block]
            )

        def after_conv(rows):
            value, slope = gelu_parts(wide[rows, :] + bias_row)
            gelleds[block, rows, :] = value.astype(BF16)
            hidden_slopes[block, rows, :] = slope

        over_rows(total, after_conv)
        sources[block + 1] = (
            sources[block].astype(F32) + dot(gelleds[block], project[...])
        ).astype(BF16)

    out_copies = leaving(0, sources.at[2])
    wait_all(y_copies + late_copies)

    def add(k, value):
        sums[k] = sums[k] + value if last else value

    for block in (1, 0):
        taps_t, project_t = late_held[2 * block : 2 * block + 2]
        hop = hops[block]
        cut = hop * tile
        add(4 * block + 3, row_dot(gelleds[block], grad[...]))
        wide[...] = dot(grad[...], project_t[...])

        def hidden_rows(rows):
            hidden_grad[rows, :] = (wide[rows, :] * hidden_slopes[block, rows, :]).astype(BF16)

        over_rows(total, hidden_rows)
        add(4 * block, row_dot(acts[block, : total - cut, :], hidden_grad[cut:, :]))
        add(4 * block + 1, row_dot(acts[block], hidden_grad[...]))
        add(4 * block + 2, row_dot(acts[block, cut:, :], hidden_grad[: total - cut, :]))
        for p in range(n):
            wide[pl.ds(p * tile, tile), :] = conv_at(hidden_grad, tile, taps_t, p, n, hop)

        def source_rows(rows):
            weighted = wide[rows, :] * norm_slopes[block, rows, :]
            x = sources[block, rows, :].astype(F32)
            inv = inverse_rms(x)
            unit = x * inv
            mean = jnp.mean(unit * weighted, axis=-1, keepdims=True)
            grad[rows, :] = (
                grad[rows, :].astype(F32) + inv * (weighted - unit * mean)
            ).astype(BF16)

        over_rows(total, source_rows)

    out_copies += leaving(1, grad)
    if last:
        keep_out[...] = sums[pl.ds(4 * core, 4)]
        send_out[...] = sums[pl.ds(4 * (1 - core), 4)].astype(BF16)
    wait_all(out_copies)


def run_chunk(inputs, cotangent, pieces, weights, late, before, hops, chunk):
    n, (_, rows, width) = len(pieces) + 1, pieces[0].shape
    last = before is not None
    total = n * rows
    full = jax.ShapeDtypeStruct((8, width, width), F32)
    half = (4, width, width)
    sums = [jax.ShapeDtypeStruct(half, F32), jax.ShapeDtypeStruct(half, BF16)] if last else [full]
    operands = [inputs, cotangent, *pieces, *weights, *late] + ([before] if last else [])
    scratch = [pltpu.VMEM(full.shape, F32)] if last else []
    outs = pl.pallas_call(
        functools.partial(chunk_kernel, n, hops, chunk, last),
        name="chunk",
        in_specs=in_place(n + 1)
        + [pl.BlockSpec(weight.shape, None) for weight in weights]
        + in_place(5 if last else 4),
        out_specs=in_place(n) + [pl.BlockSpec(kind.shape, None) for kind in sums],
        out_shape=[jax.ShapeDtypeStruct(pieces[0].shape, BF16)] * n + sums,
        scratch_shapes=scratch
        + [
            pltpu.VMEM((3, total, width), BF16),
            pltpu.VMEM((total, width), BF16),
            pltpu.VMEM((total, width), F32),
            pltpu.VMEM((total, width), BF16),
            pltpu.VMEM((2, total, width), BF16),
            pltpu.VMEM((2, total, width), BF16),
            pltpu.VMEM((2, total, width), F32),
            pltpu.VMEM((2, total, width), F32),
        ]
        + [pltpu.VMEM(weight.shape, BF16) for weight in late]
        + [pltpu.SemaphoreType.DMA((4, n)), pltpu.SemaphoreType.DMA((5,))],
        compiler_params=pltpu.CompilerParams(vmem_limit_bytes=VMEM_LIMIT),
        cost_estimate=small_cost(),
    )(*operands)
    return list(outs[:n]), list(outs[n:])


def take(array, index):
    return lax.dynamic_index_in_dim(array, index, 0, keepdims=False)


def swap(values, axis, s=1):
    return lax.ppermute(values, axis, [(i, i ^ s) for i in range(lax.axis_size(axis))])


def spread(array, me):
    n = array.shape[0]
    return [swap(take(array, me ^ s), "chain", s) for s in range(1, n)]


def assemble(pieces, me):
    out = jnp.stack(pieces)
    return jnp.take(out, me ^ jnp.arange(len(pieces)), axis=0)


def on_device(
    inputs,
    cotangent,
    taps_first,
    taps_second,
    bias_first,
    bias_second,
    proj_first,
    proj_second,
    gain_first,
    gain_second,
):
    n = lax.axis_size("chain")
    place, pair = lax.axis_index("chain"), lax.axis_index("pair")
    hops = (1, HOP2 // HOP1)
    shape = inputs.shape
    width = shape[-1]
    weight_scale = 1.0 / math.sqrt(shape[0] * shape[1] * n * HOP1)
    rows = shape[0] * shape[1] // (CHUNKS * n)
    inputs = inputs.reshape(CHUNKS * n, rows, width)
    cotangent = cotangent.reshape(CHUNKS * n, rows, width)
    flat = (3 * width, width)
    weights = (
        taps_first.reshape(flat), bias_first[None], proj_first, gain_first[None],
        taps_second.reshape(flat), bias_second[None], proj_second, gain_second[None],
    )
    late = (
        taps_first[::-1].transpose(0, 2, 1).reshape(flat), proj_first.T,
        taps_second[::-1].transpose(0, 2, 1).reshape(flat), proj_second.T,
    )

    third = max(1, (n - 1) // 3)
    far, middle, near = (
        range(n - third, n), range(n - 2 * third, n - third), range(1, n - 2 * third)
    )
    order = [s for part in (far, middle, near) for s in reversed(part)]

    picked = [
        dict(zip(part, pick(inputs, cotangent, n, chunk, part)))
        for chunk, part in ((0, order[:third]), (0, order[third:]), (1, order))
    ]
    picked = [{**picked[0], **picked[1]}, picked[2]]
    first = {s: swap(picked[0][s], "chain", s) for s in order}
    second = {}
    for s in order:
        block = picked[1][s]
        if s in middle:
            partner = s + third
            first[partner], block = lax.optimization_barrier((first[partner], block))
        second[s] = swap(block, "chain", s)
    first = [first[s] for s in range(1, n)]
    second = [second[s] for s in range(1, n)]

    def tie(pieces, part, value):
        held = [pieces[s] for s in part]
        held, value = lax.optimization_barrier((held, value))
        for s, piece in zip(part, held):
            pieces[s] = piece
        return value

    def send_back(pieces):
        return pieces[:1] + [swap(pieces[s], "chain", s) for s in range(1, n)]

    pieces, before = run_chunk(inputs, cotangent, first, weights, late, None, hops, 0)
    pieces, second = lax.optimization_barrier((pieces, second))
    results_a = send_back(pieces)
    pieces, (keep, send) = run_chunk(
        inputs, cotangent, second, weights, late, before[0], hops, 1
    )
    results_b = send_back(pieces)

    send = tie(results_a, far, send)
    got = jnp.concatenate([swap(part, "core") for part in jnp.split(send.reshape(4 * width, width), 1)])
    got = got.reshape(keep.shape)
    half = (keep + got).reshape(2, 2 * width, width)
    parts = jnp.split(take(half, 1 - pair).astype(BF16), 4)
    got = jnp.concatenate([swap(part, "pair") for part in parts])
    quarter = (take(half, pair) + got).reshape(n, 2 * width // n, width)
    quarter = tie(results_a, middle, quarter)
    got = spread(quarter.astype(BF16), place)
    total = take(quarter, place)
    for part in got:
        total = total + part
    total = (total * weight_scale).astype(BF16)
    total = tie(results_b, far, total)
    total = tie(results_a, near, total)
    own = assemble([total] + [swap(total, "chain", s) for s in range(1, n)], place)
    own = own.reshape(2 * width, width)
    by_pair, by_core = swap(own, "pair"), swap(own, "core")
    partial = put(results_a, 0, None)
    by_both = lax.ppermute(own, ("pair", "core"), [(i, i ^ 3) for i in range(4)])
    sums = finish((own, by_pair, by_core, by_both), width)
    sums, partial = lax.optimization_barrier((sums, partial))
    outputs, input_grad = put(results_b, 1, partial)
    return (outputs.reshape(shape), input_grad.reshape(shape), *sums)


def solution(mesh):
    groups, seq = mesh.shape["groups"], mesh.shape["seq"]
    own = Mesh(
        mesh.devices.reshape(groups, seq // HOP1, HOP1 // 2, 2),
        ("groups", "chain", "pair", "core"),
    )
    split = P("groups", ("chain", "pair", "core"), None)
    return jax.shard_map(
        on_device,
        mesh=own,
        in_specs=(split, split) + (P(),) * 8,
        out_specs=(
            split,
            split,
            P("groups", None, None),
            P("groups", None, None),
            P("groups", None),
            P("groups", None),
        ),
        check_vma=False,
    )
```

```python
import functools
import math

import jax
import jax.numpy as jnp
from jax import lax
from jax.experimental import pallas as pl
from jax.experimental.pallas import tpu as pltpu
from jax.sharding import Mesh
from jax.sharding import PartitionSpec as P

HOP1 = 4
HOP2 = 8

GELU_COEF = 0.7978845608028654
CUBIC = 0.044715
CHUNKS = 2
VMEM_LIMIT = 60 << 20
BF16 = jnp.bfloat16
F32 = jnp.float32


def gelu_parts(v):
    square = v * v
    th = jnp.tanh(v * (GELU_COEF + (GELU_COEF * CUBIC) * square))
    half = 0.5 + 0.5 * th
    value = v * half
    slope = half + value * (1.0 - th) * (GELU_COEF + (3.0 * CUBIC * GELU_COEF) * square)
    return value, slope


def inverse_rms(x):
    return lax.rsqrt(jnp.mean(x * x, axis=-1, keepdims=True) + 1e-06)


def dot(left, right):
    return jnp.dot(left, right, preferred_element_type=F32)


def row_dot(left, right):
    return lax.dot_general(left, right, (((0,), (0,)), ((), ())), preferred_element_type=F32)


def conv_at(parts, tile, taps, p, n, hop):
    width = parts.shape[-1]
    low = 0 if p - hop >= 0 else 1
    high = 3 if p + hop < n else 2
    left = jnp.concatenate(
        [parts[pl.ds((p + (k - 1) * hop) * tile, tile), :] for k in range(low, high)], axis=-1
    )
    return dot(left, taps[low * width : high * width, :])


def over_rows(total, body, step=64):
    for start in range(0, total, step):
        body(pl.ds(start, step))


def start_all(copies):
    for copy in copies:
        copy.start()
    return copies


def wait_all(copies):
    for copy in copies:
        copy.wait()


def stage(moves, held, sems):
    into, out = [], []
    for i, (source, target) in enumerate(moves):
        into.append(pltpu.make_async_copy(source, held.at[i], sems.at[0, i]))
        out.append(pltpu.make_async_copy(held.at[i], target, sems.at[1, i]))
    start_all(into)
    for arrival, departure in zip(into, out):
        arrival.wait()
        departure.start()
    wait_all(out)


def pick_kernel(n, chunk, order, inputs, cotangent, *refs):
    pieces, (held, sems) = refs[:-2], refs[-2:]
    me = lax.axis_index("chain")
    moves = [
        (source.at[chunk * n + (me ^ s)], pieces[i].at[k])
        for i, s in enumerate(order)
        for k, source in enumerate((inputs, cotangent))
    ]
    stage(moves, held, sems)


def pick(inputs, cotangent, n, chunk, order):
    _, rows, width = inputs.shape
    piece = jax.ShapeDtypeStruct((2, rows, width), BF16)
    return pl.pallas_call(
        functools.partial(pick_kernel, n, chunk, order),
        name="pick",
        in_specs=in_place(2),
        out_specs=in_place(len(order)),
        out_shape=[piece] * len(order),
        scratch_shapes=[
            pltpu.VMEM((2 * len(order), rows, width), BF16),
            pltpu.SemaphoreType.DMA((2, 2 * len(order))),
        ],
        cost_estimate=small_cost(),
    )(inputs, cotangent)


def put_kernel(n, chunk, order, fresh, *refs):
    count = len(order)
    pieces, refs = refs[:count], refs[count if fresh else count + 2 :]
    outs, (held, sems) = refs[:2], refs[2:]
    me = lax.axis_index("chain")
    moves = [
        (pieces[i].at[k], outs[k].at[chunk * n + (me ^ s)])
        for i, s in enumerate(order)
        for k in range(2)
    ]
    stage(moves, held, sems)


def put(pieces, chunk, into, order):
    n, (_, rows, width) = len(pieces), pieces[0].shape
    pieces, count = [pieces[s] for s in order], len(order)
    full = jax.ShapeDtypeStruct((CHUNKS * n, rows, width), BF16)
    return pl.pallas_call(
        functools.partial(put_kernel, n, chunk, order, into is None),
        name="put",
        in_specs=in_place(count if into is None else count + 2),
        out_specs=in_place(2),
        out_shape=[full, full],
        input_output_aliases={} if into is None else {count: 0, count + 1: 1},
        scratch_shapes=[
            pltpu.VMEM((2 * count, rows, width), BF16),
            pltpu.SemaphoreType.DMA((2, 2 * count)),
        ],
        compiler_params=pltpu.CompilerParams(vmem_limit_bytes=8 << 20),
        cost_estimate=pl.CostEstimate(
            flops=0, bytes_accessed=16 * count * rows * width, transcendentals=0
        ),
    )(*pieces, *(into or ()))


def finish_kernel(own, by_pair, by_core, by_both, *refs):
    outs, held, sems = refs[:4], refs[4], refs[5]
    pair, core = lax.axis_index("pair"), lax.axis_index("core")
    places = ((core, pair), (core, 1 - pair), (1 - core, pair), (1 - core, 1 - pair))
    wait_all(
        start_all(
            [
                pltpu.make_async_copy(quarter, held.at[block, half], sems.at[i])
                for i, (quarter, (block, half)) in enumerate(
                    zip((own, by_pair, by_core, by_both), places)
                )
            ]
        )
    )
    for block in range(2):
        taps, project = outs[block], outs[2 + block]
        taps[0] = held[block, 0, 0].astype(F32)
        taps[1] = held[block, 0, 1].astype(F32)
        taps[2] = held[block, 1, 0].astype(F32)
        project[...] = held[block, 1, 1].astype(F32)


def finish(quarters, width):
    quarters = [quarter.reshape(2, width, width) for quarter in quarters]
    taps = jax.ShapeDtypeStruct((3, width, width), F32)
    project = jax.ShapeDtypeStruct((width, width), F32)
    return pl.pallas_call(
        finish_kernel,
        name="finish",
        in_specs=in_place(4),
        out_shape=[taps, taps, project, project],
        scratch_shapes=[
            pltpu.VMEM((2, 2, 2, width, width), BF16),
            pltpu.SemaphoreType.DMA((4,)),
        ],
        compiler_params=pltpu.CompilerParams(vmem_limit_bytes=8 << 20),
        cost_estimate=small_cost(),
    )(*quarters)


def in_place(count):
    return [pl.BlockSpec(memory_space=pl.ANY)] * count


def small_cost():
    return pl.CostEstimate(flops=1000, bytes_accessed=1000, transcendentals=0)


def chunk_kernel(n, hops, chunk, last, *refs):
    inputs, cotangent, refs = refs[0], refs[1], refs[2:]
    pieces, weights, late, refs = refs[: n - 1], refs[n - 1 : n + 7], refs[n + 7 : n + 11], refs[n + 11 :]
    if last:
        before, refs = refs[0], refs[1:]
    piece_outs, refs = refs[:n], refs[n:]
    if last:
        keep_out, send_out, sums = refs[:3]
        refs = refs[3:]
    else:
        sums, refs = refs[0], refs[1:]
    sources, grad, wide, hidden_grad, acts, gelleds, norm_slopes, hidden_slopes = refs[:8]
    late_held, sems, late_sems = refs[8:12], refs[12], refs[13]
    me, core = lax.axis_index("chain"), lax.axis_index("core")
    _, rows_in, width = inputs.shape
    tile, total = rows_in, n * rows_in

    def place(s):
        return pl.ds(pl.multiple_of((me ^ s) * tile, tile), tile)

    def arriving(k, held, whole_array):
        copies = []
        for s in range(n):
            source = whole_array.at[chunk * n + me] if s == 0 else pieces[s - 1].at[k]
            copies.append(pltpu.make_async_copy(source, held.at[place(s), :], sems.at[k, s]))
        return start_all(copies)

    def leaving(k, held):
        copies = []
        for s in range(n):
            copies.append(
                pltpu.make_async_copy(
                    held.at[place(s), :], piece_outs[s].at[k], sems.at[2 + k, s]
                )
            )
        return start_all(copies)

    x_copies = arriving(0, sources.at[0], inputs)
    late_copies = start_all(
        [
            pltpu.make_async_copy(source, held, late_sems.at[i])
            for i, (source, held) in enumerate(zip(late, late_held))
        ]
    )
    y_copies = arriving(1, grad, cotangent)
    if last:
        late_copies += start_all([pltpu.make_async_copy(before, sums, late_sems.at[4])])
    wait_all(x_copies)

    for block in range(2):
        taps, bias, project, gain = weights[4 * block : 4 * block + 4]
        gain_row, bias_row = gain[...], bias[...]

        def before_conv(rows):
            x = sources[block, rows, :].astype(F32)
            value, slope = gelu_parts(x * inverse_rms(x) * gain_row)
            acts[block, rows, :] = value.astype(BF16)
            norm_slopes[block, rows, :] = slope * gain_row

        over_rows(total, before_conv)
        for p in range(n):
            wide[pl.ds(p * tile, tile), :] = conv_at(
                acts.at[block], tile, taps, p, n, hops[block]
            )

        def after_conv(rows):
            value, slope = gelu_parts(wide[rows, :] + bias_row)
            gelleds[block, rows, :] = value.astype(BF16)
            hidden_slopes[block, rows, :] = slope

        over_rows(total, after_conv)
        sources[block + 1] = (
            sources[block].astype(F32) + dot(gelleds[block], project[...])
        ).astype(BF16)

    out_copies = leaving(0, sources.at[2])
    wait_all(y_copies + late_copies)

    def add(k, value):
        sums[k] = sums[k] + value if last else value

    for block in (1, 0):
        taps_t, project_t = late_held[2 * block : 2 * block + 2]
        hop = hops[block]
        cut = hop * tile
        add(4 * block + 3, row_dot(gelleds[block], grad[...]))
        wide[...] = dot(grad[...], project_t[...])

        def hidden_rows(rows):
            hidden_grad[rows, :] = (wide[rows, :] * hidden_slopes[block, rows, :]).astype(BF16)

        over_rows(total, hidden_rows)
        add(4 * block, row_dot(acts[block, : total - cut, :], hidden_grad[cut:, :]))
        add(4 * block + 1, row_dot(acts[block], hidden_grad[...]))
        add(4 * block + 2, row_dot(acts[block, cut:, :], hidden_grad[: total - cut, :]))
        for p in range(n):
            wide[pl.ds(p * tile, tile), :] = conv_at(hidden_grad, tile, taps_t, p, n, hop)

        def source_rows(rows):
            weighted = wide[rows, :] * norm_slopes[block, rows, :]
            x = sources[block, rows, :].astype(F32)
            inv = inverse_rms(x)
            unit = x * inv
            mean = jnp.mean(unit * weighted, axis=-1, keepdims=True)
            grad[rows, :] = (
                grad[rows, :].astype(F32) + inv * (weighted - unit * mean)
            ).astype(BF16)

        over_rows(total, source_rows)

    out_copies += leaving(1, grad)
    if last:
        keep_out[...] = sums[pl.ds(4 * core, 4)]
        send_out[...] = sums[pl.ds(4 * (1 - core), 4)].astype(BF16)
    wait_all(out_copies)


def run_chunk(inputs, cotangent, pieces, weights, late, before, hops, chunk):
    n, (_, rows, width) = len(pieces) + 1, pieces[0].shape
    last = before is not None
    total = n * rows
    full = jax.ShapeDtypeStruct((8, width, width), F32)
    half = (4, width, width)
    sums = [jax.ShapeDtypeStruct(half, F32), jax.ShapeDtypeStruct(half, BF16)] if last else [full]
    operands = [inputs, cotangent, *pieces, *weights, *late] + ([before] if last else [])
    scratch = [pltpu.VMEM(full.shape, F32)] if last else []
    outs = pl.pallas_call(
        functools.partial(chunk_kernel, n, hops, chunk, last),
        name="chunk",
        in_specs=in_place(n + 1)
        + [pl.BlockSpec(weight.shape, None) for weight in weights]
        + in_place(5 if last else 4),
        out_specs=in_place(n) + [pl.BlockSpec(kind.shape, None) for kind in sums],
        out_shape=[jax.ShapeDtypeStruct(pieces[0].shape, BF16)] * n + sums,
        scratch_shapes=scratch
        + [
            pltpu.VMEM((3, total, width), BF16),
            pltpu.VMEM((total, width), BF16),
            pltpu.VMEM((total, width), F32),
            pltpu.VMEM((total, width), BF16),
            pltpu.VMEM((2, total, width), BF16),
            pltpu.VMEM((2, total, width), BF16),
            pltpu.VMEM((2, total, width), F32),
            pltpu.VMEM((2, total, width), F32),
        ]
        + [pltpu.VMEM(weight.shape, BF16) for weight in late]
        + [pltpu.SemaphoreType.DMA((4, n)), pltpu.SemaphoreType.DMA((5,))],
        compiler_params=pltpu.CompilerParams(vmem_limit_bytes=VMEM_LIMIT),
        cost_estimate=small_cost(),
    )(*operands)
    return list(outs[:n]), list(outs[n:])


def take(array, index):
    return lax.dynamic_index_in_dim(array, index, 0, keepdims=False)


def swap(values, axis, s=1):
    return lax.ppermute(values, axis, [(i, i ^ s) for i in range(lax.axis_size(axis))])


def spread(array, me):
    n = array.shape[0]
    return [swap(take(array, me ^ s), "chain", s) for s in range(1, n)]


def assemble(pieces, me):
    out = jnp.stack(pieces)
    return jnp.take(out, me ^ jnp.arange(len(pieces)), axis=0)


def on_device(
    inputs,
    cotangent,
    taps_first,
    taps_second,
    bias_first,
    bias_second,
    proj_first,
    proj_second,
    gain_first,
    gain_second,
):
    n = lax.axis_size("chain")
    place, pair = lax.axis_index("chain"), lax.axis_index("pair")
    hops = (1, HOP2 // HOP1)
    shape = inputs.shape
    width = shape[-1]
    weight_scale = 1.0 / math.sqrt(shape[0] * shape[1] * n * HOP1)
    rows = shape[0] * shape[1] // (CHUNKS * n)
    inputs = inputs.reshape(CHUNKS * n, rows, width)
    cotangent = cotangent.reshape(CHUNKS * n, rows, width)
    flat = (3 * width, width)
    weights = (
        taps_first.reshape(flat), bias_first[None], proj_first, gain_first[None],
        taps_second.reshape(flat), bias_second[None], proj_second, gain_second[None],
    )
    late = (
        taps_first[::-1].transpose(0, 2, 1).reshape(flat), proj_first.T,
        taps_second[::-1].transpose(0, 2, 1).reshape(flat), proj_second.T,
    )

    third = max(1, (n - 1) // 3)
    far, middle, near = (
        range(n - third, n), range(n - 2 * third, n - third), range(1, n - 2 * third)
    )
    order = [s for part in (far, middle, near) for s in reversed(part)]

    picked = [
        dict(zip(part, pick(inputs, cotangent, n, chunk, part)))
        for chunk, part in ((0, order[:third]), (0, order[third:]), (1, order))
    ]
    picked = [{**picked[0], **picked[1]}, picked[2]]
    first = {s: swap(picked[0][s], "chain", s) for s in order}
    second = {}
    for s in order:
        block = picked[1][s]
        if s in middle:
            partner = s + third
            first[partner], block = lax.optimization_barrier((first[partner], block))
        second[s] = swap(block, "chain", s)
    first = [first[s] for s in range(1, n)]
    second = [second[s] for s in range(1, n)]

    def tie(pieces, part, value):
        held = [pieces[s] for s in part]
        held, value = lax.optimization_barrier((held, value))
        for s, piece in zip(part, held):
            pieces[s] = piece
        return value

    def send_back(pieces):
        return pieces[:1] + [swap(pieces[s], "chain", s) for s in range(1, n)]

    pieces, before = run_chunk(inputs, cotangent, first, weights, late, None, hops, 0)
    pieces, second = lax.optimization_barrier((pieces, second))
    results_a = send_back(pieces)
    pieces, (keep, send) = run_chunk(
        inputs, cotangent, second, weights, late, before[0], hops, 1
    )
    results_b = send_back(pieces)

    send = tie(results_a, far, send)
    got = jnp.concatenate([swap(part, "core") for part in jnp.split(send.reshape(4 * width, width), 1)])
    got = got.reshape(keep.shape)
    half = (keep + got).reshape(2, 2 * width, width)
    parts = jnp.split(take(half, 1 - pair).astype(BF16), 4)
    got = jnp.concatenate([swap(part, "pair") for part in parts])
    quarter = (take(half, pair) + got).reshape(n, 2 * width // n, width)
    quarter = tie(results_a, middle, quarter)
    got = spread(quarter.astype(BF16), place)
    total = take(quarter, place)
    for part in got:
        total = total + part
    total = (total * weight_scale).astype(BF16)
    total = tie(results_b, far, total)
    total = tie(results_a, near, total)
    own = assemble([total] + [swap(total, "chain", s) for s in range(1, n)], place)
    own = own.reshape(2 * width, width)
    by_pair, by_core = swap(own, "pair"), swap(own, "core")
    partial = put(results_a, 0, None, range(n))
    by_both = lax.ppermute(own, ("pair", "core"), [(i, i ^ 3) for i in range(4)])
    sums = finish((own, by_pair, by_core, by_both), width)
    partial = put(results_b, 1, partial, [0, *far])
    sums, partial = lax.optimization_barrier((sums, partial))
    outputs, input_grad = put(results_b, 1, partial, [*near, *middle])
    return (outputs.reshape(shape), input_grad.reshape(shape), *sums)


def solution(mesh):
    groups, seq = mesh.shape["groups"], mesh.shape["seq"]
    own = Mesh(
        mesh.devices.reshape(groups, seq // HOP1, HOP1 // 2, 2),
        ("groups", "chain", "pair", "core"),
    )
    split = P("groups", ("chain", "pair", "core"), None)
    return jax.shard_map(
        on_device,
        mesh=own,
        in_specs=(split, split) + (P(),) * 8,
        out_specs=(
            split,
            split,
            P("groups", None, None),
            P("groups", None, None),
            P("groups", None),
            P("groups", None),
        ),
        check_vma=False,
    )
```
